256 devices in a mesh: mem: 16 (over y, x), tile: 16 (over z, core).
Axes of the slice: x: 4, y: 4, z: 8, core: 2. Of those that a mesh axis runs over, the one named last changes fastest.
Arguments:
- ensemble: float32 [1024, 3, 128, 256], P('mem', None, 'tile'), may hold values from -4.5 to 5
- obs_cells: int32 [16, 256], replicated, may hold values from 0 to 6143
- region_tile: int32 [16], replicated, may hold values from 0 to 15, each once
- obs_values: float32 [16, 256], replicated, may hold values from -5.6 to 5.6
- obs_error: float32 [16, 256], replicated, may hold values from 0.05 to 0.75
Outputs:
- analysis: float32 [1024, 3, 128, 256], P('mem', None, 'tile')
The draws below stay inside these ranges and needn't reach their ends.
Inputs may be any that keep to these rules, and one draw needn't show every extreme that they name: `obs_cells`: row r lists flat indices into the values of tile region_tile[r], ordered by field, then row within the tile, then column; indices may repeat. `region_tile`: each tile holds exactly one region.
All inputs are finite; a program needn't handle non-finite values.
Results may differ from the reference program's by a relative error of at most 0.00029.
Values sent between devices are 32-bit elements; how exact they have to be, the bound alone decides.
A program may use at most 64 MiB of HBM per device.

```python
import math
import jax
import jax.numpy as jnp
from jax import lax

ENSEMBLE_SIZE = 1024
MESH_LONGITUDES = 256
BLOCK_LATITUDES = 8
OBS = 256
STEPS = 4
DEGREE = 4
GY = 128
VALS_T = 6144
REGION_TOTAL = 16
N_MEM = 16
N_TILE = 16


def draw_ensemble(key, part):
    sample = jnp.clip(jax.random.normal(key, (ENSEMBLE_SIZE, 3, GY, MESH_LONGITUDES), jnp.float32), -3.0, 3.0)
    return 0.5 * sample


def draw_obs_values(key, part):
    position = jnp.arange(REGION_TOTAL, dtype=jnp.float32) / max(REGION_TOTAL - 1, 1)
    sample = jnp.clip(jax.random.normal(key, (REGION_TOTAL, OBS), jnp.float32), -3.0, 3.0)
    return sample * jnp.sqrt(1.0 + 2.0 * position)[:, None]


def draw_obs_error(key, part):
    rising = 1.0 + 2.0 * jnp.arange(REGION_TOTAL, dtype=jnp.float32) / max(REGION_TOTAL - 1, 1)
    sample = jnp.exp(jax.random.uniform(key, (REGION_TOTAL, OBS), jnp.float32, math.log(0.05), math.log(0.25)))
    return sample * rising[:, None]


def with_ends(array, stream_key, low, top_value):
    longest = array.shape.index(max(array.shape))
    spots = []
    for shift in (0, 1):
        where = [jax.random.randint(jax.random.fold_in(stream_key, axis), (), 0, length) for axis, length in enumerate(array.shape)]
        where[longest] = (where[longest] + shift) % array.shape[longest]
        spots.append(tuple(where))
    return array.at[spots[0]].set(low).at[spots[1]].set(top_value)


def setup_inputs(seed: int = 0) -> dict:
    splits = jax.random.split(jax.random.key(seed), 6)
    return {
        "ensemble": draw_ensemble(jax.random.fold_in(splits[5], 71), 0),
        "obs_cells": with_ends(jax.random.randint(splits[1], (REGION_TOTAL, OBS), 0, VALS_T), jax.random.fold_in(splits[1], 1), 0, VALS_T - 1).astype(jnp.int32),
        "region_tile": jax.random.permutation(splits[2], N_TILE).astype(jnp.int32),
        "obs_values": draw_obs_values(jax.random.fold_in(splits[5], 71), 0),
        "obs_error": draw_obs_error(jax.random.fold_in(splits[5], 71), 0),
    }


DEPTH = 1.0
GRAVITY = 1.0
CORIOLIS = 0.5
TIMESTEP = 0.3
DIFFUSE = 0.1
PRECISE = lax.Precision.HIGHEST

def east_diff(quantity):
    return 0.5 * (jnp.roll(quantity, -1, axis=-1) - jnp.roll(quantity, 1, axis=-1))

def north_diff(quantity):
    return 0.5 * (quantity[:, 2:] - quantity[:, :-2])

def interior(quantity):
    return quantity[:, 1:-1]

def smoothing(quantity):
    middle = interior(quantity)
    return jnp.roll(middle, -1, axis=-1) + jnp.roll(middle, 1, axis=-1) + quantity[:, 2:] + quantity[:, :-2] - 4.0 * middle

def advance(padded):
    height = padded[:, 0]
    eastward = padded[:, 1]
    northward = padded[:, 2]
    height_mid = interior(height)
    east_mid = interior(eastward)
    north_mid = interior(northward)
    column = DEPTH + height
    height_rate = -(interior(east_diff(column * eastward)) + north_diff(column * northward))
    east_rate = -(east_mid * interior(east_diff(eastward)) + north_mid * north_diff(eastward)) - GRAVITY * interior(east_diff(height)) + CORIOLIS * north_mid
    north_rate = -(east_mid * interior(east_diff(northward)) + north_mid * north_diff(northward)) - GRAVITY * north_diff(height) - CORIOLIS * east_mid
    return jnp.stack([height_mid + TIMESTEP * height_rate + DIFFUSE * smoothing(height), east_mid + TIMESTEP * east_rate + DIFFUSE * smoothing(eastward), north_mid + TIMESTEP * north_rate + DIFFUSE * smoothing(northward)], axis=1)

def predicted_prior(ensemble_block):
    for repeat in range(STEPS):
        ensemble_block = advance(jnp.pad(ensemble_block, ((0, 0), (0, 0), (1, 1), (0, 0)), mode='wrap'))
    return ensemble_block

def innovations(observed, target, variance, weight):
    obs_mean = lax.optimization_barrier(jnp.mean(observed, axis=0))
    perturbed = (observed - obs_mean) * weight
    misfit = (target - obs_mean) * weight
    spread = lax.optimization_barrier(jnp.sum(perturbed * perturbed, axis=0)) / (observed.shape[0] - 1)
    return (perturbed, misfit, jnp.sum(misfit * misfit), jnp.sum(weight * (spread + variance)))

def gram_terms(perturbed, misfit, variance):
    weighted_matrix = perturbed / variance
    product = jnp.einsum('mo,no->mn', weighted_matrix, perturbed, precision=PRECISE)
    projected = jnp.dot(perturbed, misfit / variance, precision=PRECISE)
    return (product, projected)

def spectral_map(gram_scaled):
    upper_bound = 2.0 + jnp.sqrt(jnp.sum(gram_scaled * gram_scaled))
    order_count = gram_scaled.shape[0]
    shifted = 2.0 / (upper_bound - 1.0) * gram_scaled - jnp.eye(order_count, dtype=jnp.float32)
    orders = jnp.arange(DEGREE + 1, dtype=jnp.float32)
    angles = (orders + 0.5) * (math.pi / (DEGREE + 1))
    levels = 0.5 * (upper_bound + 1.0) + 0.5 * (upper_bound - 1.0) * jnp.cos(angles)
    values = lax.rsqrt(levels)
    cos_table = jnp.cos(orders[:, None] * angles[None, :])
    coeffs = 2.0 / (DEGREE + 1) * lax.optimization_barrier(jnp.sum(cos_table * values[None, :], axis=1))
    coeffs = coeffs * jnp.where(orders == 0.0, 0.5, 1.0)
    return (shifted, coeffs)

def chebyshev(shifted, operand, coeffs):
    previous = operand
    current = jnp.dot(shifted, operand, precision=PRECISE)
    summed = coeffs[0] * previous + coeffs[1] * current
    for term_index in range(2, DEGREE + 1):
        following = 2.0 * jnp.dot(shifted, current, precision=PRECISE) - previous
        summed = summed + coeffs[term_index] * following
        previous, current = (current, following)
    return summed

def analyse(columns, product, projected, inflation):
    gram_scaled = inflation / (ENSEMBLE_SIZE - 1) * product
    shifted, coeffs = spectral_map(gram_scaled)
    centre = lax.optimization_barrier(jnp.mean(columns, axis=0))
    spread = columns - centre
    shaped = chebyshev(shifted, spread, coeffs)
    weights = inflation / (ENSEMBLE_SIZE - 1) * chebyshev(shifted, chebyshev(shifted, projected, coeffs), coeffs)
    mean_shift = jnp.dot(weights, spread, precision=PRECISE)
    return centre + jnp.sqrt(inflation) * shaped + mean_shift

def reference(ensemble, obs_cells, region_tile, obs_values, obs_error):
    ensemble_block = ensemble.reshape(N_MEM, ENSEMBLE_SIZE // N_MEM, 3, GY, MESH_LONGITUDES)
    layered_arrays = lax.map(predicted_prior, ensemble_block).reshape(ENSEMBLE_SIZE, 3, N_TILE, BLOCK_LATITUDES, MESH_LONGITUDES)
    by_tile = jnp.transpose(layered_arrays, (2, 0, 1, 3, 4)).reshape(N_TILE, ENSEMBLE_SIZE, 3 * BLOCK_LATITUDES * MESH_LONGITUDES)
    region_count = region_tile.shape[0]
    tile_region = jnp.zeros((region_count,), jnp.int32).at[region_tile].set(jnp.arange(region_count, dtype=jnp.int32))
    obs_index = obs_cells[tile_region]
    targets = obs_values[tile_region]
    variances = obs_error[tile_region]
    unit = jnp.ones((OBS,), jnp.float32)

    def tile_sums(packed):
        flat_state, index_row, target, variance = packed
        observed = jnp.take(flat_state, index_row, axis=1)
        perturbed, misfit, misfit_sum, spread_sum = innovations(observed, target, variance, unit)
        return (misfit_sum, spread_sum)
    misfit_sums, spread_sums = lax.map(tile_sums, (by_tile, obs_index, targets, variances))
    inflation = jnp.sum(misfit_sums) / jnp.sum(spread_sums)

    def tile_update(packed):
        flat_state, index_row, target, variance = packed
        observed = jnp.take(flat_state, index_row, axis=1)
        perturbed, misfit, misfit_sum, spread_sum = innovations(observed, target, variance, unit)
        product, projected = gram_terms(perturbed, misfit, variance)
        return analyse(flat_state, product, projected, inflation)
    updated = lax.map(tile_update, (by_tile, obs_index, targets, variances))
    return jnp.transpose(updated.reshape(N_TILE, ENSEMBLE_SIZE, 3, BLOCK_LATITUDES, MESH_LONGITUDES), (1, 2, 0, 3, 4)).reshape(ENSEMBLE_SIZE, 3, GY, MESH_LONGITUDES)
```

```python
import math

import jax
import jax.numpy as jnp
from jax import lax
from jax.sharding import PartitionSpec as P

ENSEMBLE_SIZE = 1024
STEPS = 4
DEGREE = 4


DEPTH = 1.0
GRAVITY = 1.0
CORIOLIS = 0.5
TIMESTEP = 0.3
DIFFUSE = 0.1
PRECISE = lax.Precision.HIGHEST


def with_halo(cells, sides, width):
    for axis, dim in sides:
        count = lax.axis_size(axis)
        head = lax.slice_in_dim(cells, 0, width, axis=dim)
        tail = lax.slice_in_dim(cells, cells.shape[dim] - width, cells.shape[dim], axis=dim)
        cells = jnp.concatenate(
            [
                lax.ppermute(tail, axis, [(i, (i + 1) % count) for i in range(count)]),
                cells,
                lax.ppermute(head, axis, [((i + 1) % count, i) for i in range(count)]),
            ],
            axis=dim,
        )
    return cells


def laid_out(tiles, dim):
    tiles = jnp.moveaxis(tiles, 0, dim)
    shape = tiles.shape
    return tiles.reshape(*shape[:dim], shape[dim] * shape[dim + 1], *shape[dim + 2 :])


def sent_to_all(value, axis):
    copies = jnp.broadcast_to(value, (lax.axis_size(axis), *value.shape))
    return lax.all_to_all(copies, axis, split_axis=0, concat_axis=0, tiled=True)


def gather_directly(value, axis, dim):
    return laid_out(sent_to_all(value, axis), dim)


def over_copies(value, axis):
    everything = sent_to_all(value, axis)
    return jnp.sum(everything, axis=0)


def in_one(arrays, axis):
    vector, at, outs = (jnp.concatenate([a.reshape(-1) for a in arrays]), 0, [])
    subtotal = over_copies(vector, axis)
    for a in arrays:
        outs.append(subtotal[at : at + a.size].reshape(a.shape))
        at += a.size
    return tuple(outs)


def east_diff(quantity):
    return 0.5 * (jnp.roll(quantity, -1, axis=-1) - jnp.roll(quantity, 1, axis=-1))


def north_diff(quantity):
    return 0.5 * (quantity[:, 2:] - quantity[:, :-2])


def interior(quantity):
    return quantity[:, 1:-1]


def smoothing(quantity):
    middle = interior(quantity)
    return (
        jnp.roll(middle, -1, axis=-1)
        + jnp.roll(middle, 1, axis=-1)
        + quantity[:, 2:]
        + quantity[:, :-2]
        - 4.0 * middle
    )


def advance(padded):
    height = padded[:, 0]
    eastward = padded[:, 1]
    northward = padded[:, 2]
    height_mid = interior(height)
    east_mid = interior(eastward)
    north_mid = interior(northward)
    column = DEPTH + height
    height_rate = -(interior(east_diff(column * eastward)) + north_diff(column * northward))
    east_rate = (
        -(east_mid * interior(east_diff(eastward)) + north_mid * north_diff(eastward))
        - GRAVITY * interior(east_diff(height))
        + CORIOLIS * north_mid
    )
    north_rate = (
        -(east_mid * interior(east_diff(northward)) + north_mid * north_diff(northward))
        - GRAVITY * north_diff(height)
        - CORIOLIS * east_mid
    )
    return jnp.stack(
        [
            height_mid + TIMESTEP * height_rate + DIFFUSE * smoothing(height),
            east_mid + TIMESTEP * east_rate + DIFFUSE * smoothing(eastward),
            north_mid + TIMESTEP * north_rate + DIFFUSE * smoothing(northward),
        ],
        axis=1,
    )


def innovations(observed, target, variance, weight):
    obs_mean = jnp.mean(observed, axis=0)
    perturbed = (observed - obs_mean) * weight
    misfit = (target - obs_mean) * weight
    spread = jnp.sum(perturbed * perturbed, axis=0) / (observed.shape[0] - 1)
    return (perturbed, misfit, jnp.sum(misfit * misfit), jnp.sum(weight * (spread + variance)))


def spectral_map(norm):
    upper_bound = 2.0 + norm
    orders = jnp.arange(DEGREE + 1, dtype=jnp.float32)
    angles = (orders + 0.5) * (math.pi / (DEGREE + 1))
    levels = 0.5 * (upper_bound + 1.0) + 0.5 * (upper_bound - 1.0) * jnp.cos(angles)
    values = lax.rsqrt(levels)
    cos_table = jnp.cos(orders[:, None] * angles[None, :])
    coeffs = 2.0 / (DEGREE + 1) * jnp.sum(cos_table * values[None, :], axis=1)
    coeffs = coeffs * jnp.where(orders == 0.0, 0.5, 1.0)
    return (2.0 / (upper_bound - 1.0), coeffs)


def matmul(a, b):
    return jnp.dot(a, b, precision=PRECISE)


def analyse(columns, scaled, goal, inflation):
    gain = inflation / (ENSEMBLE_SIZE - 1)
    inner = jnp.einsum("mo,mq->oq", scaled, scaled, precision=PRECISE)
    scale, c = spectral_map(gain * jnp.sqrt(jnp.sum(inner * inner)))
    eye = jnp.eye(inner.shape[0], dtype=jnp.float32)
    lifted = scale * gain * inner
    a = lifted - eye
    a2 = matmul(a, a)
    r = (
        c[1] * eye
        + 2.0 * c[2] * (a - eye)
        + c[3] * (4.0 * (a2 - a) + eye)
        + 8.0 * c[4] * (matmul(a2, a) - a2)
    )
    p0 = c[0] - c[1] + c[2] - c[3] + c[4]
    centre = jnp.mean(columns, axis=0)
    spread = columns - centre
    cross = jnp.einsum("mo,mc->oc", scaled, spread, precision=PRECISE)
    h = goal[None, :]
    for _ in range(2):
        h = p0 * h + matmul(matmul(h, r), lifted)
    mean_shift = gain * matmul(h, cross)[0]
    root = jnp.sqrt(inflation)
    moved = matmul(scaled, (root * scale * gain) * matmul(r, cross))
    return centre + (root * p0 * spread + moved) + mean_shift


def on_device(ensemble, obs_cells, region_tile, obs_values, obs_error):
    layered_arrays = with_halo(ensemble, (("tile", 2),), STEPS)
    for repeat in range(STEPS):
        layered_arrays = advance(layered_arrays)
    chosen = (region_tile == lax.axis_index("tile"))[:, None]
    obs_index = jnp.sum(jnp.where(chosen, obs_cells, 0), axis=0)
    target = jnp.sum(jnp.where(chosen, obs_values, 0.0), axis=0)
    variance = jnp.sum(jnp.where(chosen, obs_error, 0.0), axis=0)
    flat_state = layered_arrays.reshape(layered_arrays.shape[0], -1)
    selected_entries = jnp.take(flat_state, obs_index, axis=1)
    observed = gather_directly(selected_entries, "mem", 0)
    columns = lax.all_to_all(flat_state, "mem", split_axis=1, concat_axis=0, tiled=True)
    unit = jnp.ones(target.shape, jnp.float32)
    perturbed, misfit, misfit_sum, spread_sum = innovations(observed, target, variance, unit)
    misfit_sum, spread_sum = in_one((misfit_sum, spread_sum), "tile")
    inflation = misfit_sum / spread_sum
    weight = lax.rsqrt(variance)
    updated = analyse(columns, perturbed * weight, misfit * weight, inflation)
    restored_fields = lax.all_to_all(updated, "mem", split_axis=0, concat_axis=1, tiled=True)
    return restored_fields.reshape(ensemble.shape)


def solution(mesh):
    in_specs = (P("mem", None, "tile", None), P(), P(), P(), P())
    out_specs = P("mem", None, "tile", None)
    return jax.shard_map(
        on_device, mesh=mesh, in_specs=in_specs, out_specs=out_specs, check_vma=False
    )
```

```python
import functools
import math

import jax
import jax.numpy as jnp
from jax import lax
from jax.experimental import pallas as pl
from jax.experimental.pallas import tpu as pltpu
from jax.sharding import PartitionSpec as P

MEMBERS = 1024
STEPS = 4
DEGREE = 4
SIDE = 4
N_MEM = 16
N_TILE = 16
ROWS = 8
LONS = 256
LANES = 128
OBS = 256
OWN = MEMBERS // N_MEM
COLS = 3 * LANES
CHUNK = 16
CHUNKS = OWN // CHUNK
GROUP = SIDE * OWN

MESH = pl.DeviceIdType.MESH
F32, BF16 = jnp.float32, jnp.bfloat16

FAR_FIRST = (2, 1, 3, 0)
OFFSETS = [(dy, dx) for dy in FAR_FIRST for dx in FAR_FIRST if (dy, dx) != (0, 0)]


def dot(a, b):
    return jnp.dot(a, b, preferred_element_type=F32)


def split(a):
    high = a.astype(BF16)
    return high, (a - high.astype(F32)).astype(BF16)


def dot_split(ah, al, bh, bl):
    return dot(ah, bh) + (dot(ah, bl) + dot(al, bh))


def matmul(a, b):
    return dot_split(*split(a), *split(b))


def total(a):
    return jnp.sum(jnp.sum(a, axis=0, keepdims=True), axis=1, keepdims=True)


def advanced(load):
    h, u, v = load(0, 1), load(1, 1), load(2, 1)
    hs, us, vs = load(0, 0), load(1, 0), load(2, 0)
    hn, un, vn = load(0, 2), load(1, 2), load(2, 2)
    he, hw = pltpu.roll(h, LONS - 1, 1), pltpu.roll(h, 1, 1)
    ue, uw = pltpu.roll(u, LONS - 1, 1), pltpu.roll(u, 1, 1)
    ve, vw = pltpu.roll(v, LONS - 1, 1), pltpu.roll(v, 1, 1)
    flux = ((1.0 + he) * ue - (1.0 + hw) * uw) + ((1.0 + hn) * vn - (1.0 + hs) * vs)
    push_u = u * (ue - uw) + v * (un - us) + (he - hw) - v
    push_v = u * (ve - vw) + v * (vn - vs) + (hn - hs) + u
    return (
        0.6 * h + 0.1 * ((he + hw) + (hn + hs)) - 0.15 * flux,
        0.6 * u + 0.1 * ((ue + uw) + (un + us)) - 0.15 * push_u,
        0.6 * v + 0.1 * ((ve + vw) + (vn + vs)) - 0.15 * push_v,
    )


def spectral_map(norm):
    bound = 2.0 + norm
    values = []
    for j in range(DEGREE + 1):
        angle = (j + 0.5) * (math.pi / (DEGREE + 1))
        values.append(lax.rsqrt(0.5 * (bound + 1.0) + (0.5 * math.cos(angle)) * (bound - 1.0)))
    coeffs = []
    for k in range(DEGREE + 1):
        factor = 2.0 / (DEGREE + 1) * (0.5 if k == 0 else 1.0)
        terms = [
            (factor * math.cos(k * (j + 0.5) * (math.pi / (DEGREE + 1)))) * values[j]
            for j in range(DEGREE + 1)
        ]
        coeffs.append(sum(terms[1:], terms[0]))
    return 2.0 / (bound - 1.0), coeffs


def kernel(
    state, slab_ref, lane_ref, goal_ref, error_ref, out,
    wide, ping, pong, outgoing, seen, columns, observed, sums_out, sums_in,
    uth, utl, uh, ul, dh, dl, result,
    load_sem, halo_send, halo_recv, obs_send, obs_recv, col_send, col_recv,
    sum_send, sum_recv, back_send, back_recv,
):
    me = lax.axis_index("mem")
    tile = lax.axis_index("tile")
    mine_y, mine_x = me // SIDE, lax.rem(me, SIDE)
    above, below = lax.rem(tile + 1, N_TILE), lax.rem(tile + N_TILE - 1, N_TILE)

    def peer(dy, dx):
        return lax.rem(mine_y + dy, SIDE) * SIDE + lax.rem(mine_x + dx, SIDE)

    def members(c):
        return pl.ds(pl.multiple_of(c * CHUNK, CHUNK), CHUNK)

    def block(i):
        return pl.ds(pl.multiple_of(i * OWN, OWN), OWN)

    def load_copy(c):
        part = members(c)
        return pltpu.make_async_copy(
            state.at[:, :, part, :], wide.at[:, STEPS : STEPS + ROWS, part, :], load_sem.at[c]
        )

    def halo_copy(c, side):
        part = members(c)
        first, into, to = ((ROWS - STEPS, 0, above), (0, STEPS + ROWS, below))[side]
        return pltpu.make_async_remote_copy(
            src_ref=state.at[:, first : first + STEPS, part, :],
            dst_ref=wide.at[:, into : into + STEPS, part, :],
            send_sem=halo_send.at[side, c],
            recv_sem=halo_recv.at[side, c],
            device_id={"tile": to},
            device_id_type=MESH,
        )

    def obs_copy(c, n, to):
        return pltpu.make_async_remote_copy(
            src_ref=seen.at[members(c), :],
            dst_ref=observed.at[pl.ds(pl.multiple_of(me * OWN + c * CHUNK, CHUNK), CHUNK), :],
            send_sem=obs_send.at[n],
            recv_sem=obs_recv.at[me],
            device_id={"mem": to},
            device_id_type=MESH,
        )

    def col_copy(n, to):
        return pltpu.make_async_remote_copy(
            src_ref=outgoing.at[to],
            dst_ref=columns.at[block(me), :],
            send_sem=col_send.at[n],
            recv_sem=col_recv.at[me],
            device_id={"mem": to},
            device_id_type=MESH,
        )

    def sum_copy(n, to):
        return pltpu.make_async_remote_copy(
            src_ref=sums_out,
            dst_ref=sums_in.at[tile],
            send_sem=sum_send.at[n],
            recv_sem=sum_recv.at[tile],
            device_id={"tile": to},
            device_id_type=MESH,
        )

    def back_copy(n, to):
        return pltpu.make_async_remote_copy(
            src_ref=result.at[block(to), :],
            dst_ref=out.at[me],
            send_sem=back_send.at[n],
            recv_sem=back_recv.at[me],
            device_id={"mem": to},
            device_id_type=MESH,
        )

    def wait_for(ref, sem):
        pltpu.make_async_copy(ref, ref, sem).wait()

    for c in range(CHUNKS):
        load_copy(c).start()
    barrier = pltpu.get_barrier_semaphore()
    for dy, dx in OFFSETS:
        pl.semaphore_signal(barrier, inc=1, device_id={"mem": peer(dy, dx)}, device_id_type=MESH)
    for k in range(1, N_TILE):
        to = lax.rem(tile + k, N_TILE)
        pl.semaphore_signal(barrier, inc=1, device_id={"tile": to}, device_id_type=MESH)
    pl.semaphore_wait(barrier, N_MEM + N_TILE - 2)
    for c in range(CHUNKS):
        halo_copy(c, 0).start()
        halo_copy(c, 1).start()

    def forecast(c, carry):
        part = members(c)
        load_copy(c).wait()
        wait_for(wide.at[:, 0:STEPS, part, :], halo_recv.at[0, c])
        wait_for(wide.at[:, 0:STEPS, part, :], halo_recv.at[1, c])

        def step(count, read, write):
            def row(i, carry):
                new = advanced(lambda f, k: read(f, i + k))
                for f in range(3):
                    write[f, i] = new[f]
                return carry

            lax.fori_loop(0, count, row, 0)

        step(ROWS + 6, lambda f, i: wide[f, i, part, :], ping)
        step(ROWS + 4, lambda f, i: ping[f, i], pong)
        step(ROWS + 2, lambda f, i: pong[f, i], ping)

        def last(i, found):
            new = advanced(lambda f, k: ping[f, i + k])
            found = list(found)
            for f in range(3):
                for half in range(2):
                    values = new[f][:, half * LANES : (half + 1) * LANES]
                    outgoing[2 * i + half, part, f * LANES : (f + 1) * LANES] = values
                    slab = f * (2 * ROWS) + 2 * i + half
                    for g in range(2):
                        lanes = slice(g * LANES, (g + 1) * LANES)
                        here = slab_ref[:, lanes] == slab
                        for s in range(CHUNK // 8):
                            n = g * (CHUNK // 8) + s
                            taken = jnp.take_along_axis(
                                values[s * 8 : s * 8 + 8], lane_ref[:, lanes], axis=1
                            )
                            found[n] = jnp.where(here, taken, found[n])
            return tuple(found)

        none = jnp.zeros((8, LANES), F32)
        found = lax.fori_loop(0, ROWS, last, (none,) * (2 * (CHUNK // 8)))
        for g in range(2):
            for s in range(CHUNK // 8):
                at = pl.multiple_of(c * CHUNK + s * 8, 8)
                seen[pl.ds(at, 8), g * LANES : (g + 1) * LANES] = found[g * (CHUNK // 8) + s]
        for n, (dy, dx) in enumerate(OFFSETS):
            obs_copy(c, n, peer(dy, dx)).start()
        return carry

    lax.fori_loop(0, CHUNKS, forecast, 0)
    for n, (dy, dx) in enumerate(OFFSETS):
        col_copy(n, peer(dy, dx)).start()
    observed[block(me), :] = seen[...]
    columns[block(me), :] = outgoing[me]

    for dy, dx in OFFSETS:
        src = peer(dy, dx)
        wait_for(observed.at[block(src), :], obs_recv.at[src])
    obs_mean = jnp.sum(observed[...], axis=0, keepdims=True) * (1.0 / MEMBERS)
    error = error_ref[...]
    weight = lax.rsqrt(error)
    misfit = goal_ref[...] - obs_mean
    square = jnp.zeros((1, OBS), F32)
    for b in range(MEMBERS // LANES):
        rows = slice(b * LANES, (b + 1) * LANES)
        centred = observed[rows, :] - obs_mean
        square = square + jnp.sum(centred * centred, axis=0, keepdims=True)
        scaled = centred * weight
        uh[rows, :], ul[rows, :] = split(scaled)
        uth[:, rows], utl[:, rows] = split(scaled.T)
    misfit_sum = total(misfit * misfit)
    spread_sum = total(square * (1.0 / (MEMBERS - 1)) + error)
    upper = lax.broadcasted_iota(jnp.int32, (8, LANES), 0) < 4
    sums_out[...] = jnp.where(upper, misfit_sum, spread_sum)
    for k in range(1, N_TILE):
        sum_copy(k, lax.rem(tile + k, N_TILE)).start()
    sums_in[tile] = sums_out[...]
    inner = dot_split(uth[...], utl[...], uh[...], ul[...])
    norm = jnp.sqrt(total(inner * inner))
    for k in range(1, N_TILE):
        src = lax.rem(tile + k, N_TILE)
        wait_for(sums_in.at[src], sum_recv.at[src])
    sums = jnp.sum(sums_in[...], axis=0)
    inflation = sums[0:1, 0:1] / sums[4:5, 0:1]

    gain = inflation * (1.0 / (MEMBERS - 1))
    root = jnp.sqrt(inflation)
    scale, c = spectral_map(gain * norm)
    p0 = c[0] - c[1] + c[2] - c[3] + c[4]
    eye = (
        lax.broadcasted_iota(jnp.int32, (OBS, OBS), 0)
        == lax.broadcasted_iota(jnp.int32, (OBS, OBS), 1)
    ).astype(F32)
    lifted = (scale * gain) * inner
    a = lifted - eye
    a2 = matmul(a, a)
    a3 = matmul(a2, a)
    r = (
        c[1] * eye
        + (2.0 * c[2]) * (a - eye)
        + c[3] * (4.0 * (a2 - a) + eye)
        + (8.0 * c[4]) * (a3 - a2)
    )
    lifted_split = split(lifted)
    r_split = split(r)
    h = jnp.broadcast_to(misfit * weight, (8, OBS))
    for _ in range(2):
        h = p0 * h + dot_split(*split(dot_split(*split(h), *r_split)), *lifted_split)
    h_split = split(gain * h)

    for dy, dx in OFFSETS:
        src = peer(dy, dx)
        wait_for(columns.at[block(src), :], col_recv.at[src])
    centre = jnp.sum(columns[...], axis=0, keepdims=True) * (1.0 / MEMBERS)
    for b in range(MEMBERS // LANES):
        rows = slice(b * LANES, (b + 1) * LANES)
        dh[rows, :], dl[rows, :] = split(columns[rows, :] - centre)
    cross_split = split(dot_split(uth[...], utl[...], dh[...], dl[...]))
    moved_split = split((root * scale * gain) * dot_split(*r_split, *cross_split))
    base = centre + dot_split(*h_split, *cross_split)[0:1, :]
    keep = root * p0
    order = {offset: n for n, offset in enumerate(OFFSETS)}
    for dy in FAR_FIRST:
        q = lax.rem(mine_y + dy, SIDE)
        rows = pl.ds(pl.multiple_of(q * GROUP, GROUP), GROUP)
        shift = dot_split(uh[rows, :], ul[rows, :], *moved_split)
        result[rows, :] = base + (keep * (columns[rows, :] - centre) + shift)
        for dx in FAR_FIRST:
            if (dy, dx) in order:
                back_copy(order[dy, dx], peer(dy, dx)).start()
    out[me] = result[block(me), :]

    for n, (dy, dx) in enumerate(OFFSETS):
        src = peer(dy, dx)
        wait_for(out.at[src], back_recv.at[src])
    for c in range(CHUNKS):
        halo_copy(c, 0).wait_send()
        halo_copy(c, 1).wait_send()
    for n, (dy, dx) in enumerate(OFFSETS):
        to = peer(dy, dx)
        wait_for(seen, obs_send.at[n])
        col_copy(n, to).wait_send()
        back_copy(n, to).wait_send()
    for k in range(1, N_TILE):
        sum_copy(k, lax.rem(tile + k, N_TILE)).wait_send()


def on_device(ensemble, obs_cells, region_tile, obs_values, obs_error):
    chosen = (region_tile == lax.axis_index("tile"))[:, None]
    cells = jnp.sum(jnp.where(chosen, obs_cells, 0), axis=0)
    goal = jnp.sum(jnp.where(chosen, obs_values, 0.0), axis=0)[None, :]
    error = jnp.sum(jnp.where(chosen, obs_error, 0.0), axis=0)[None, :]
    slab = jnp.broadcast_to(cells // LANES, (8, OBS))
    lane = jnp.broadcast_to(cells % LANES, (8, OBS))
    state = jnp.transpose(ensemble, (1, 2, 0, 3))
    vmem = pl.BlockSpec(memory_space=pltpu.VMEM)
    dma = pltpu.SemaphoreType.DMA
    updated = pl.pallas_call(
        kernel,
        name="analysis",
        out_shape=jax.ShapeDtypeStruct((N_MEM, OWN, COLS), F32),
        in_specs=[pl.BlockSpec(memory_space=pl.ANY), vmem, vmem, vmem, vmem],
        out_specs=vmem,
        scratch_shapes=[
            pltpu.VMEM((3, ROWS + 2 * STEPS, OWN, LONS), F32),
            pltpu.VMEM((3, ROWS + 6, CHUNK, LONS), F32),
            pltpu.VMEM((3, ROWS + 4, CHUNK, LONS), F32),
            pltpu.VMEM((N_MEM, OWN, COLS), F32),
            pltpu.VMEM((OWN, OBS), F32),
            pltpu.VMEM((MEMBERS, COLS), F32),
            pltpu.VMEM((MEMBERS, OBS), F32),
            pltpu.VMEM((8, LANES), F32),
            pltpu.VMEM((N_TILE, 8, LANES), F32),
            pltpu.VMEM((OBS, MEMBERS), BF16),
            pltpu.VMEM((OBS, MEMBERS), BF16),
            pltpu.VMEM((MEMBERS, OBS), BF16),
            pltpu.VMEM((MEMBERS, OBS), BF16),
            pltpu.VMEM((MEMBERS, COLS), BF16),
            pltpu.VMEM((MEMBERS, COLS), BF16),
            pltpu.VMEM((MEMBERS, COLS), F32),
            dma((CHUNKS,)),
            dma((2, CHUNKS)),
            dma((2, CHUNKS)),
            dma((N_MEM,)),
            dma((N_MEM,)),
            dma((N_MEM,)),
            dma((N_MEM,)),
            dma((N_TILE,)),
            dma((N_TILE,)),
            dma((N_MEM,)),
            dma((N_MEM,)),
        ],
        compiler_params=pltpu.CompilerParams(
            collective_id=0, has_side_effects=True, vmem_limit_bytes=44 << 20
        ),
    )(state, slab, lane, goal, error)
    updated = updated.reshape(ROWS, 2, OWN, 3, LANES)
    return jnp.transpose(updated, (2, 3, 0, 1, 4)).reshape(ensemble.shape)


def solution(mesh):
    in_specs = (P("mem", None, "tile", None), P(), P(), P(), P())
    out_specs = P("mem", None, "tile", None)
    return jax.shard_map(
        on_device, mesh=mesh, in_specs=in_specs, out_specs=out_specs, check_vma=False
    )
```

```python
import functools
import math

import jax
import jax.numpy as jnp
from jax import lax
from jax.experimental import pallas as pl
from jax.experimental.pallas import tpu as pltpu
from jax.sharding import PartitionSpec as P

MEMBERS = 1024
STEPS = 4
DEGREE = 4
SIDE = 4
N_MEM = 16
N_TILE = 16
ROWS = 8
LONS = 256
LANES = 128
OBS = 256
OWN = MEMBERS // N_MEM
LINES = 3 * ROWS
COLS = 3 * LANES
CHUNK = 8
CHUNKS = OWN // CHUNK
GROUP = SIDE * OWN

MESH = pl.DeviceIdType.MESH
F32, BF16 = jnp.float32, jnp.bfloat16

PARTNERS = [(dy, (dy + k) % SIDE) for k in (2, 1, 3, 0) for dy in (2, 1, 3, 0)]
BACK = [PARTNERS.index((-dy % SIDE, -dx % SIDE)) for dy, dx in PARTNERS]
OTHERS = range(N_MEM - 1)
SELF = N_MEM - 1
ARRIVAL = (0, 2, 1, 3)
EARLY = 2


def dot(a, b):
    return jnp.dot(a, b, preferred_element_type=F32)


def split(a):
    high = a.astype(BF16)
    return high, (a - high.astype(F32)).astype(BF16)


def dot_split(ah, al, bh, bl):
    return dot(ah, bh) + (dot(ah, bl) + dot(al, bh))


def matmul(a, b):
    return dot_split(*split(a), *split(b))


def total(a):
    return jnp.sum(jnp.sum(a, axis=0, keepdims=True), axis=1, keepdims=True)


def advanced(load):
    h, u, v = load(0, 1), load(1, 1), load(2, 1)
    hs, us, vs = load(0, 0), load(1, 0), load(2, 0)
    hn, un, vn = load(0, 2), load(1, 2), load(2, 2)
    he, hw = pltpu.roll(h, LONS - 1, 1), pltpu.roll(h, 1, 1)
    ue, uw = pltpu.roll(u, LONS - 1, 1), pltpu.roll(u, 1, 1)
    ve, vw = pltpu.roll(v, LONS - 1, 1), pltpu.roll(v, 1, 1)
    flux = ((1.0 + he) * ue - (1.0 + hw) * uw) + ((1.0 + hn) * vn - (1.0 + hs) * vs)
    push_u = u * (ue - uw) + v * (un - us) + (he - hw) - v
    push_v = u * (ve - vw) + v * (vn - vs) + (hn - hs) + u
    return (
        0.6 * h + 0.1 * ((he + hw) + (hn + hs)) - 0.15 * flux,
        0.6 * u + 0.1 * ((ue + uw) + (un + us)) - 0.15 * push_u,
        0.6 * v + 0.1 * ((ve + vw) + (vn + vs)) - 0.15 * push_v,
    )


def spectral_map(norm):
    bound = 2.0 + norm
    values = []
    for j in range(DEGREE + 1):
        angle = (j + 0.5) * (math.pi / (DEGREE + 1))
        values.append(lax.rsqrt(0.5 * (bound + 1.0) + (0.5 * math.cos(angle)) * (bound - 1.0)))
    coeffs = []
    for k in range(DEGREE + 1):
        factor = 2.0 / (DEGREE + 1) * (0.5 if k == 0 else 1.0)
        terms = [
            (factor * math.cos(k * (j + 0.5) * (math.pi / (DEGREE + 1)))) * values[j]
            for j in range(DEGREE + 1)
        ]
        coeffs.append(sum(terms[1:], terms[0]))
    return 2.0 / (bound - 1.0), coeffs


def kernel(
    state, cells_in, region_in, goals_in, errors_in, out,
    cells_ref, region_ref, goals_ref, errors_ref, raw, wide, ping, pong, slab_ref, lane_ref, outgoing, seen, columns, observed, sums_out, sums_in,
    uth, utl, uh, ul, cross, result, returned, ready,
    small_sem, load_sem, halo_send, halo_recv, obs_send, obs_recv, col_send, col_recv,
    sum_send, sum_recv, back_send, back_recv, out_sem,
):
    me = lax.axis_index("mem")
    tile = lax.axis_index("tile")
    mine_y, mine_x = me // SIDE, lax.rem(me, SIDE)
    above, below = lax.rem(tile + 1, N_TILE), lax.rem(tile + N_TILE - 1, N_TILE)

    def peer(n):
        dy, dx = PARTNERS[n]
        return lax.rem(mine_y + dy, SIDE) * SIDE + lax.rem(mine_x + dx, SIDE)

    def members(c):
        return pl.ds(pl.multiple_of(c * CHUNK, CHUNK), CHUNK)

    def block(n):
        return slice(n * OWN, (n + 1) * OWN)

    def load_copy(c):
        part = pl.ds(c * CHUNK * LINES, CHUNK * LINES)
        return [
            pltpu.make_async_copy(
                state.at[part, half * LANES : (half + 1) * LANES],
                raw.at[half, part, :],
                load_sem.at[c, half],
            )
            for half in range(2)
        ]

    def halo_copy(c, side):
        part = members(c)
        first, into, to = ((ROWS, 0, above), (STEPS, STEPS + ROWS, below))[side]
        return pltpu.make_async_remote_copy(
            src_ref=wide.at[:, first : first + STEPS, part, :],
            dst_ref=wide.at[:, into : into + STEPS, part, :],
            send_sem=halo_send.at[side, c],
            recv_sem=halo_recv.at[side, c],
            device_id={"tile": to},
            device_id_type=MESH,
        )

    def obs_copy(n, c, chunks):
        count = chunks * CHUNK
        first = pl.multiple_of(c * CHUNK, CHUNK)
        return pltpu.make_async_remote_copy(
            src_ref=seen.at[pl.ds(first, count), :],
            dst_ref=observed.at[pl.ds(BACK[n] * OWN + first, count), :],
            send_sem=obs_send.at[n],
            recv_sem=obs_recv.at[BACK[n]],
            device_id={"mem": peer(n)},
            device_id_type=MESH,
        )

    def col_copy(n, c, chunks):
        count = chunks * CHUNK
        first = pl.multiple_of(c * CHUNK, CHUNK)
        return pltpu.make_async_remote_copy(
            src_ref=outgoing.at[peer(n), pl.ds(first, count), :],
            dst_ref=columns.at[pl.ds(BACK[n] * OWN + first, count), :],
            send_sem=col_send.at[n],
            recv_sem=col_recv.at[BACK[n]],
            device_id={"mem": peer(n)},
            device_id_type=MESH,
        )

    def sum_copy(n, to):
        return pltpu.make_async_remote_copy(
            src_ref=sums_out,
            dst_ref=sums_in.at[tile],
            send_sem=sum_send.at[n],
            recv_sem=sum_recv.at[tile],
            device_id={"tile": to},
            device_id_type=MESH,
        )

    def back_copy(n):
        return pltpu.make_async_remote_copy(
            src_ref=result.at[block(n), :],
            dst_ref=returned.at[me],
            send_sem=back_send.at[n],
            recv_sem=back_recv.at[me],
            device_id={"mem": peer(n)},
            device_id_type=MESH,
        )

    def wait_for(ref, sem):
        pltpu.make_async_copy(ref, ref, sem).wait()

    small = [
        pltpu.make_async_copy(src, dst, small_sem.at[n])
        for n, (src, dst) in enumerate(
            [
                (region_in, region_ref),
                (cells_in, cells_ref),
                (goals_in, goals_ref),
                (errors_in, errors_ref),
            ]
        )
    ]
    for c in range(CHUNKS):
        for copy in load_copy(c):
            copy.start()
    for copy in small:
        copy.start()
    barrier = pltpu.get_barrier_semaphore()
    for n in OTHERS:
        pl.semaphore_signal(barrier, inc=1, device_id={"mem": peer(n)}, device_id_type=MESH)
    for k in range(1, N_TILE):
        to = lax.rem(tile + k, N_TILE)
        pl.semaphore_signal(barrier, inc=1, device_id={"tile": to}, device_id_type=MESH)

    for copy in small:
        copy.wait()
    cells = jnp.zeros((1, OBS), jnp.int32)
    goal = jnp.zeros((1, OBS), F32)
    error = jnp.zeros((1, OBS), F32)
    for region in range(N_TILE):
        chosen = region_ref[region] == tile
        cells = jnp.where(chosen, cells_ref[region : region + 1, :], cells)
        goal = jnp.where(chosen, goals_ref[region : region + 1, :], goal)
        error = jnp.where(chosen, errors_ref[region : region + 1, :], error)
    cells = jnp.broadcast_to(cells, (8, OBS))
    slab_ref[...] = lax.shift_right_logical(cells, 7)
    lane_ref[...] = lax.bitwise_and(cells, LANES - 1)
    for c in range(CHUNKS):
        for copy in load_copy(c):
            copy.wait()
        for m in range(c * CHUNK, (c + 1) * CHUNK, 8):
            for f in range(3):
                for i in range(ROWS):
                    first = m * LINES + f * ROWS + i
                    for half in range(2):
                        lanes = slice(half * LANES, (half + 1) * LANES)
                        wide[f, STEPS + i, m : m + 8, lanes] = raw[
                            half, pl.ds(first, 8, stride=LINES), :
                        ]
    pl.semaphore_wait(barrier, N_MEM + N_TILE - 2)
    for c in range(CHUNKS):
        halo_copy(c, 0).start()
        halo_copy(c, 1).start()

    def forecast(c, carry):
        part = members(c)
        wait_for(wide.at[:, 0:STEPS, part, :], halo_recv.at[0, c])
        wait_for(wide.at[:, 0:STEPS, part, :], halo_recv.at[1, c])

        def step(count, read, write):
            for i in range(count):
                new = advanced(lambda f, k: read(f, i + k))
                for f in range(3):
                    write[f, i] = new[f]

        step(ROWS + 6, lambda f, i: wide[f, i, part, :], ping)
        step(ROWS + 4, lambda f, i: ping[f, i], pong)
        step(ROWS + 2, lambda f, i: pong[f, i], ping)

        found = [jnp.zeros((8, LANES), F32)] * (2 * (CHUNK // 8))
        for i in range(ROWS):
            new = advanced(lambda f, k: ping[f, i + k])
            for f in range(3):
                for half in range(2):
                    values = new[f][:, half * LANES : (half + 1) * LANES]
                    outgoing[2 * i + half, part, f * LANES : (f + 1) * LANES] = values
                    slab = f * (2 * ROWS) + 2 * i + half
                    for g in range(2):
                        lanes = slice(g * LANES, (g + 1) * LANES)
                        here = slab_ref[:, lanes] == slab
                        for s in range(CHUNK // 8):
                            n = g * (CHUNK // 8) + s
                            taken = jnp.take_along_axis(
                                values[s * 8 : s * 8 + 8],
                                lane_ref[:, lanes],
                                axis=1,
                                mode="promise_in_bounds",
                            )
                            found[n] = jnp.where(here, taken, found[n])
        for g in range(2):
            for s in range(CHUNK // 8):
                at = pl.multiple_of(c * CHUNK + s * 8, 8)
                seen[pl.ds(at, 8), g * LANES : (g + 1) * LANES] = found[g * (CHUNK // 8) + s]

        @pl.when(lax.rem(c, 2) == 1)
        def _():
            for n in OTHERS:
                obs_copy(n, c - 1, 2).start()

        @pl.when(c < EARLY)
        def _():
            for n in OTHERS:
                col_copy(n, c, 1).start()

        return carry

    lax.fori_loop(0, CHUNKS, forecast, 0)
    for n in OTHERS:
        col_copy(n, EARLY, CHUNKS - EARLY).start()
    observed[block(SELF), :] = seen[...]
    columns[block(SELF), :] = outgoing[me]
    near = jnp.sum(outgoing[me], axis=0, keepdims=True) * (1.0 / OWN)

    for n in OTHERS:
        wait_for(observed.at[block(n), :], obs_recv.at[n])
    obs_mean = jnp.sum(observed[...], axis=0, keepdims=True) * (1.0 / MEMBERS)
    weight = lax.rsqrt(error)
    misfit = goal - obs_mean
    square = jnp.zeros((1, OBS), F32)
    for b in range(SIDE):
        rows = slice(b * GROUP, (b + 1) * GROUP)
        centred = observed[rows, :] - obs_mean
        square = square + jnp.sum(centred * centred, axis=0, keepdims=True)
        scaled = centred * weight
        uh[rows, :], ul[rows, :] = split(scaled)
        uth[b], utl[b] = split(scaled.T)
    misfit_sum = total(misfit * misfit)
    spread_sum = total(square * (1.0 / (MEMBERS - 1)) + error)
    upper = lax.broadcasted_iota(jnp.int32, (8, LANES), 0) < 4
    sums_out[...] = jnp.where(upper, misfit_sum, spread_sum)
    for k in range(1, N_TILE):
        sum_copy(k, lax.rem(tile + k, N_TILE)).start()
    sums_in[tile] = sums_out[...]
    inner = jnp.zeros((OBS, OBS), F32)
    for b in range(SIDE):
        rows = slice(b * GROUP, (b + 1) * GROUP)
        inner = inner + dot_split(uth[b], utl[b], uh[rows, :], ul[rows, :])
    norm = jnp.sqrt(total(inner * inner))
    for k in range(1, N_TILE):
        src = lax.rem(tile + k, N_TILE)
        wait_for(sums_in.at[src], sum_recv.at[src])
    sums = jnp.sum(sums_in[...], axis=0)
    inflation = sums[0:1, 0:1] / sums[4:5, 0:1]

    gain = inflation * (1.0 / (MEMBERS - 1))
    root = jnp.sqrt(inflation)
    scale, c = spectral_map(gain * norm)
    p0 = c[0] - c[1] + c[2] - c[3] + c[4]
    eye = (
        lax.broadcasted_iota(jnp.int32, (OBS, OBS), 0)
        == lax.broadcasted_iota(jnp.int32, (OBS, OBS), 1)
    ).astype(F32)
    lifted = (scale * gain) * inner
    a = lifted - eye
    a2 = matmul(a, a)
    a3 = matmul(a2, a)
    r = (
        c[1] * eye
        + (2.0 * c[2]) * (a - eye)
        + c[3] * (4.0 * (a2 - a) + eye)
        + (8.0 * c[4]) * (a3 - a2)
    )
    lifted_split = split(lifted)
    r_split = split(r)
    h = jnp.broadcast_to(misfit * weight, (8, OBS))
    for _ in range(2):
        h = p0 * h + dot_split(*split(dot_split(*split(h), *r_split)), *lifted_split)
    h_split = split(gain * h)

    column_sum = jnp.zeros((1, COLS), F32)
    for g in ARRIVAL:
        for n in range(g * SIDE, (g + 1) * SIDE):
            if n != SELF:
                wait_for(columns.at[block(n), :], col_recv.at[n])
        group = columns[g * GROUP : (g + 1) * GROUP, :]
        column_sum = column_sum + jnp.sum(group, axis=0, keepdims=True)
        part = dot_split(uth[g], utl[g], *split(group - near))
        cross[...] = part if g == ARRIVAL[0] else cross[...] + part
    centre = column_sum * (1.0 / MEMBERS)
    cross_split = split(cross[...])
    moved_split = split((root * scale * gain) * dot_split(*r_split, *cross_split))
    base = centre + dot_split(*h_split, *cross_split)[0:1, :]
    keep = root * p0
    for g in range(SIDE):
        rows = slice(g * GROUP, (g + 1) * GROUP)
        shift = dot_split(uh[rows, :], ul[rows, :], *moved_split)
        result[rows, :] = base + (keep * (columns[rows, :] - centre) + shift)
        for n in range(g * SIDE, (g + 1) * SIDE):
            if n != SELF:
                back_copy(n).start()
    returned[me] = result[block(SELF), :]

    finals = []
    for half in range(2):
        for i in range(ROWS):
            src = 2 * i + half

            @pl.when(src != me)
            def _():
                wait_for(returned.at[src], back_recv.at[src])

            for m in range(0, OWN, 8):
                for f in range(3):
                    ready[half, pl.ds(m * LINES + f * ROWS + i, 8, stride=LINES), :] = returned[
                        src, m : m + 8, f * LANES : (f + 1) * LANES
                    ]
        finals.append(
            pltpu.make_async_copy(
                ready.at[half], out.at[:, half * LANES : (half + 1) * LANES], out_sem.at[half]
            )
        )
        finals[-1].start()
    for c in range(CHUNKS):
        halo_copy(c, 0).wait_send()
        halo_copy(c, 1).wait_send()
    for n in OTHERS:
        wait_for(seen, obs_send.at[n])
        wait_for(outgoing.at[0], col_send.at[n])
        back_copy(n).wait_send()
    for k in range(1, N_TILE):
        sum_copy(k, lax.rem(tile + k, N_TILE)).wait_send()
    for copy in finals:
        copy.wait()


def on_device(ensemble, obs_cells, region_tile, obs_values, obs_error):
    state = ensemble.reshape(OWN * LINES, LONS)
    dma = pltpu.SemaphoreType.DMA
    updated = pl.pallas_call(
        kernel,
        name="analysis",
        out_shape=jax.ShapeDtypeStruct((OWN * LINES, LONS), F32),
        in_specs=[pl.BlockSpec(memory_space=pltpu.HBM)] * 5,
        out_specs=pl.BlockSpec(memory_space=pltpu.HBM),
        scratch_shapes=[
            pltpu.VMEM((N_TILE, OBS), jnp.int32),
            pltpu.SMEM((N_TILE,), jnp.int32),
            pltpu.VMEM((N_TILE, OBS), F32),
            pltpu.VMEM((N_TILE, OBS), F32),
            pltpu.VMEM((2, OWN * LINES, LANES), F32),
            pltpu.VMEM((3, ROWS + 2 * STEPS, OWN, LONS), F32),
            pltpu.VMEM((3, ROWS + 6, CHUNK, LONS), F32),
            pltpu.VMEM((3, ROWS + 4, CHUNK, LONS), F32),
            pltpu.VMEM((8, OBS), jnp.int32),
            pltpu.VMEM((8, OBS), jnp.int32),
            pltpu.VMEM((N_MEM, OWN, COLS), F32),
            pltpu.VMEM((OWN, OBS), F32),
            pltpu.VMEM((MEMBERS, COLS), F32),
            pltpu.VMEM((MEMBERS, OBS), F32),
            pltpu.VMEM((8, LANES), F32),
            pltpu.VMEM((N_TILE, 8, LANES), F32),
            pltpu.VMEM((SIDE, OBS, GROUP), BF16),
            pltpu.VMEM((SIDE, OBS, GROUP), BF16),
            pltpu.VMEM((MEMBERS, OBS), BF16),
            pltpu.VMEM((MEMBERS, OBS), BF16),
            pltpu.VMEM((OBS, COLS), F32),
            pltpu.VMEM((MEMBERS, COLS), F32),
            pltpu.VMEM((N_MEM, OWN, COLS), F32),
            pltpu.VMEM((2, OWN * LINES, LANES), F32),
            dma((4,)),
            dma((CHUNKS, 2)),
            dma((2, CHUNKS)),
            dma((2, CHUNKS)),
            dma((N_MEM,)),
            dma((N_MEM,)),
            dma((N_MEM,)),
            dma((N_MEM,)),
            dma((N_TILE,)),
            dma((N_TILE,)),
            dma((N_MEM,)),
            dma((N_MEM,)),
            dma((2,)),
        ],
        compiler_params=pltpu.CompilerParams(
            collective_id=0, has_side_effects=True, vmem_limit_bytes=60_000_000
        ),
    )(state, obs_cells, region_tile, obs_values, obs_error)
    return updated.reshape(ensemble.shape)


def solution(mesh):
    in_specs = (P("mem", None, "tile", None), P(), P(), P(), P())
    out_specs = P("mem", None, "tile", None)
    return jax.shard_map(
        on_device, mesh=mesh, in_specs=in_specs, out_specs=out_specs, check_vma=False
    )
```

```python
import functools
import math

import jax
import jax.numpy as jnp
from jax import lax
from jax.experimental import pallas as pl
from jax.experimental.pallas import tpu as pltpu
from jax.sharding import PartitionSpec as P

MEMBERS = 1024
STEPS = 4
DEGREE = 4
SIDE = 4
N_MEM = 16
N_TILE = 16
ROWS = 8
LONS = 256
LANES = 128
OBS = 256
OWN = MEMBERS // N_MEM
LINES = 3 * ROWS
CHUNK = 8
CHUNKS = OWN // CHUNK
GROUP = SIDE * OWN

MESH = pl.DeviceIdType.MESH
F32, BF16 = jnp.float32, jnp.bfloat16

PARTNERS = [(dy, (dy + k) % SIDE) for k in (2, 1, 3, 0) for dy in (2, 1, 3, 0)]
BACK = [PARTNERS.index((-dy % SIDE, -dx % SIDE)) for dy, dx in PARTNERS]
OTHERS = range(N_MEM - 1)
SELF = N_MEM - 1
ARRIVAL = (0, 2, 1, 3)
EARLY = 2


def dot(a, b):
    return jnp.dot(a, b, preferred_element_type=F32)


def split(a):
    high = a.astype(BF16)
    return high, (a - high.astype(F32)).astype(BF16)


def dot_split(ah, al, bh, bl):
    return dot(ah, bh) + (dot(ah, bl) + dot(al, bh))


def matmul(a, b):
    return dot_split(*split(a), *split(b))


def total(a):
    return jnp.sum(jnp.sum(a, axis=0, keepdims=True), axis=1, keepdims=True)


def advanced(load):
    h, u, v = load(0, 1), load(1, 1), load(2, 1)
    hs, us, vs = load(0, 0), load(1, 0), load(2, 0)
    hn, un, vn = load(0, 2), load(1, 2), load(2, 2)
    he, hw = pltpu.roll(h, LONS - 1, 1), pltpu.roll(h, 1, 1)
    ue, uw = pltpu.roll(u, LONS - 1, 1), pltpu.roll(u, 1, 1)
    ve, vw = pltpu.roll(v, LONS - 1, 1), pltpu.roll(v, 1, 1)
    flux = ((1.0 + he) * ue - (1.0 + hw) * uw) + ((1.0 + hn) * vn - (1.0 + hs) * vs)
    push_u = u * (ue - uw) + v * (un - us) + (he - hw) - v
    push_v = u * (ve - vw) + v * (vn - vs) + (hn - hs) + u
    return (
        0.6 * h + 0.1 * ((he + hw) + (hn + hs)) - 0.15 * flux,
        0.6 * u + 0.1 * ((ue + uw) + (un + us)) - 0.15 * push_u,
        0.6 * v + 0.1 * ((ve + vw) + (vn + vs)) - 0.15 * push_v,
    )


def spectral_map(norm):
    bound = 2.0 + norm
    values = []
    for j in range(DEGREE + 1):
        angle = (j + 0.5) * (math.pi / (DEGREE + 1))
        values.append(lax.rsqrt(0.5 * (bound + 1.0) + (0.5 * math.cos(angle)) * (bound - 1.0)))
    coeffs = []
    for k in range(DEGREE + 1):
        factor = 2.0 / (DEGREE + 1) * (0.5 if k == 0 else 1.0)
        terms = [
            (factor * math.cos(k * (j + 0.5) * (math.pi / (DEGREE + 1)))) * values[j]
            for j in range(DEGREE + 1)
        ]
        coeffs.append(sum(terms[1:], terms[0]))
    return 2.0 / (bound - 1.0), coeffs


def kernel(
    state, cells_in, region_in, goals_in, errors_in, out,
    cells_ref, region_ref, goals_ref, errors_ref, raw, wide, ping, pong, slab_ref, lane_ref, outgoing, seen, columns, observed, sums_out, sums_in,
    uth, utl, uh, ul, result, returned, ready,
    small_sem, load_sem, halo_send, halo_recv, obs_send, obs_recv, early_send, early_recv, col_send, col_recv,
    sum_send, sum_recv, back_send, back_recv, out_sem,
):
    me = lax.axis_index("mem")
    tile = lax.axis_index("tile")
    mine_y, mine_x = me // SIDE, lax.rem(me, SIDE)
    above, below = lax.rem(tile + 1, N_TILE), lax.rem(tile + N_TILE - 1, N_TILE)

    def peer(n):
        dy, dx = PARTNERS[n]
        return lax.rem(mine_y + dy, SIDE) * SIDE + lax.rem(mine_x + dx, SIDE)

    def members(c):
        return pl.ds(pl.multiple_of(c * CHUNK, CHUNK), CHUNK)

    def block(n):
        return slice(n * OWN, (n + 1) * OWN)

    def load_copy(c):
        part = pl.ds(c * CHUNK * LINES, CHUNK * LINES)
        return [
            pltpu.make_async_copy(
                state.at[part, half * LANES : (half + 1) * LANES],
                raw.at[half, part, :],
                load_sem.at[c, half],
            )
            for half in range(2)
        ]

    def halo_copy(c, side):
        part = members(c)
        first, into, to = ((ROWS, 0, above), (STEPS, STEPS + ROWS, below))[side]
        return pltpu.make_async_remote_copy(
            src_ref=wide.at[:, first : first + STEPS, part, :],
            dst_ref=wide.at[:, into : into + STEPS, part, :],
            send_sem=halo_send.at[side, c],
            recv_sem=halo_recv.at[side, c],
            device_id={"tile": to},
            device_id_type=MESH,
        )

    def obs_copy(n, c, chunks):
        count = chunks * CHUNK
        first = pl.multiple_of(c * CHUNK, CHUNK)
        return pltpu.make_async_remote_copy(
            src_ref=seen.at[pl.ds(first, count), :],
            dst_ref=observed.at[pl.ds(BACK[n] * OWN + first, count), :],
            send_sem=obs_send.at[n],
            recv_sem=obs_recv.at[BACK[n]],
            device_id={"mem": peer(n)},
            device_id_type=MESH,
        )

    def early_copy(n, c):
        first = pl.multiple_of(c * CHUNK, CHUNK)
        return pltpu.make_async_remote_copy(
            src_ref=outgoing.at[:, peer(n), pl.ds(first, CHUNK), :],
            dst_ref=columns.at[:, pl.ds(BACK[n] * OWN + first, CHUNK), :],
            send_sem=early_send.at[n],
            recv_sem=early_recv.at[BACK[n]],
            device_id={"mem": peer(n)},
            device_id_type=MESH,
        )

    def col_copy(n, f):
        count = OWN - EARLY * CHUNK
        return pltpu.make_async_remote_copy(
            src_ref=outgoing.at[f, peer(n), pl.ds(EARLY * CHUNK, count), :],
            dst_ref=columns.at[f, pl.ds(BACK[n] * OWN + EARLY * CHUNK, count), :],
            send_sem=col_send.at[f, n],
            recv_sem=col_recv.at[f, BACK[n]],
            device_id={"mem": peer(n)},
            device_id_type=MESH,
        )

    def sum_copy(n, to):
        return pltpu.make_async_remote_copy(
            src_ref=sums_out,
            dst_ref=sums_in.at[tile],
            send_sem=sum_send.at[n],
            recv_sem=sum_recv.at[tile],
            device_id={"tile": to},
            device_id_type=MESH,
        )

    def back_copy(n, f):
        return pltpu.make_async_remote_copy(
            src_ref=result.at[f, block(n), :],
            dst_ref=returned.at[f, me],
            send_sem=back_send.at[f, n],
            recv_sem=back_recv.at[f, me],
            device_id={"mem": peer(n)},
            device_id_type=MESH,
        )

    def wait_for(ref, sem):
        pltpu.make_async_copy(ref, ref, sem).wait()

    small = [
        pltpu.make_async_copy(src, dst, small_sem.at[n])
        for n, (src, dst) in enumerate(
            [
                (region_in, region_ref),
                (cells_in, cells_ref),
                (goals_in, goals_ref),
                (errors_in, errors_ref),
            ]
        )
    ]
    for c in range(CHUNKS):
        for copy in load_copy(c):
            copy.start()
    for copy in small:
        copy.start()
    barrier = pltpu.get_barrier_semaphore()
    for n in OTHERS:
        pl.semaphore_signal(barrier, inc=1, device_id={"mem": peer(n)}, device_id_type=MESH)
    for k in range(1, N_TILE):
        to = lax.rem(tile + k, N_TILE)
        pl.semaphore_signal(barrier, inc=1, device_id={"tile": to}, device_id_type=MESH)

    for copy in small:
        copy.wait()
    cells = jnp.zeros((1, OBS), jnp.int32)
    goal = jnp.zeros((1, OBS), F32)
    error = jnp.zeros((1, OBS), F32)
    for region in range(N_TILE):
        chosen = region_ref[region] == tile
        cells = jnp.where(chosen, cells_ref[region : region + 1, :], cells)
        goal = jnp.where(chosen, goals_ref[region : region + 1, :], goal)
        error = jnp.where(chosen, errors_ref[region : region + 1, :], error)
    cells = jnp.broadcast_to(cells, (8, OBS))
    slab_ref[...] = lax.shift_right_logical(cells, 7)
    lane_ref[...] = lax.bitwise_and(cells, LANES - 1)
    for c in range(CHUNKS):
        for copy in load_copy(c):
            copy.wait()
        for m in range(c * CHUNK, (c + 1) * CHUNK, 8):
            for f in range(3):
                for i in range(ROWS):
                    first = m * LINES + f * ROWS + i
                    for half in range(2):
                        lanes = slice(half * LANES, (half + 1) * LANES)
                        wide[f, STEPS + i, m : m + 8, lanes] = raw[
                            half, pl.ds(first, 8, stride=LINES), :
                        ]
    pl.semaphore_wait(barrier, N_MEM + N_TILE - 2)
    for c in range(CHUNKS):
        halo_copy(c, 0).start()
        halo_copy(c, 1).start()

    def forecast(c, carry):
        part = members(c)
        wait_for(wide.at[:, 0:STEPS, part, :], halo_recv.at[0, c])
        wait_for(wide.at[:, 0:STEPS, part, :], halo_recv.at[1, c])

        def step(count, read, write):
            for i in range(count):
                new = advanced(lambda f, k: read(f, i + k))
                for f in range(3):
                    write[f, i] = new[f]

        step(ROWS + 6, lambda f, i: wide[f, i, part, :], ping)
        step(ROWS + 4, lambda f, i: ping[f, i], pong)
        step(ROWS + 2, lambda f, i: pong[f, i], ping)

        found = [jnp.zeros((8, LANES), F32)] * (2 * (CHUNK // 8))
        for i in range(ROWS):
            new = advanced(lambda f, k: ping[f, i + k])
            for f in range(3):
                for half in range(2):
                    values = new[f][:, half * LANES : (half + 1) * LANES]
                    outgoing[f, 2 * i + half, part, :] = values
                    slab = f * (2 * ROWS) + 2 * i + half
                    for g in range(2):
                        lanes = slice(g * LANES, (g + 1) * LANES)
                        here = slab_ref[:, lanes] == slab
                        for s in range(CHUNK // 8):
                            n = g * (CHUNK // 8) + s
                            taken = jnp.take_along_axis(
                                values[s * 8 : s * 8 + 8],
                                lane_ref[:, lanes],
                                axis=1,
                                mode="promise_in_bounds",
                            )
                            found[n] = jnp.where(here, taken, found[n])
        for g in range(2):
            for s in range(CHUNK // 8):
                at = pl.multiple_of(c * CHUNK + s * 8, 8)
                seen[pl.ds(at, 8), g * LANES : (g + 1) * LANES] = found[g * (CHUNK // 8) + s]

        @pl.when(lax.rem(c, 2) == 1)
        def _():
            for n in OTHERS:
                obs_copy(n, c - 1, 2).start()

        @pl.when(c < EARLY)
        def _():
            for n in OTHERS:
                early_copy(n, c).start()

        return carry

    lax.fori_loop(0, CHUNKS, forecast, 0)
    for f in range(3):
        for n in OTHERS:
            col_copy(n, f).start()
    observed[block(SELF), :] = seen[...]
    columns[:, block(SELF), :] = outgoing[:, me]

    for n in OTHERS:
        wait_for(observed.at[block(n), :], obs_recv.at[n])
    obs_mean = jnp.sum(observed[...], axis=0, keepdims=True) * (1.0 / MEMBERS)
    weight = lax.rsqrt(error)
    misfit = goal - obs_mean
    square = jnp.zeros((1, OBS), F32)
    for b in range(SIDE):
        centred = observed[b * GROUP : (b + 1) * GROUP, :] - obs_mean
        square = square + jnp.sum(centred * centred, axis=0, keepdims=True)
    misfit_sum = total(misfit * misfit)
    spread_sum = total(square * (1.0 / (MEMBERS - 1)) + error)
    upper = lax.broadcasted_iota(jnp.int32, (8, LANES), 0) < 4
    sums_out[...] = jnp.where(upper, misfit_sum, spread_sum)
    for k in range(1, N_TILE):
        sum_copy(k, lax.rem(tile + k, N_TILE)).start()
    sums_in[tile] = sums_out[...]
    inner = jnp.zeros((OBS, OBS), F32)
    for b in range(SIDE):
        rows = slice(b * GROUP, (b + 1) * GROUP)
        scaled = (observed[rows, :] - obs_mean) * weight
        u_split = split(scaled)
        uh[rows, :], ul[rows, :] = u_split
        ut_split = split(scaled.T)
        uth[b], utl[b] = ut_split
        inner = inner + dot_split(*ut_split, *u_split)
    norm = jnp.sqrt(total(inner * inner))
    for k in range(1, N_TILE):
        src = lax.rem(tile + k, N_TILE)
        wait_for(sums_in.at[src], sum_recv.at[src])
    sums = jnp.sum(sums_in[...], axis=0)
    inflation = sums[0:1, 0:1] / sums[4:5, 0:1]

    gain = inflation * (1.0 / (MEMBERS - 1))
    root = jnp.sqrt(inflation)
    scale, c = spectral_map(gain * norm)
    p0 = c[0] - c[1] + c[2] - c[3] + c[4]
    eye = (
        lax.broadcasted_iota(jnp.int32, (OBS, OBS), 0)
        == lax.broadcasted_iota(jnp.int32, (OBS, OBS), 1)
    ).astype(F32)
    lifted = (scale * gain) * inner
    a = lifted - eye
    a_split = split(a)
    a2 = dot_split(*a_split, *a_split)
    a3 = dot_split(*split(a2), *a_split)
    r_split = split(
        c[1] * eye
        + (2.0 * c[2]) * (a - eye)
        + c[3] * (4.0 * (a2 - a) + eye)
        + (8.0 * c[4]) * (a3 - a2)
    )
    lifted_split = split(lifted)

    keep = root * p0
    for f in range(3):
        near = jnp.sum(outgoing[f, me], axis=0, keepdims=True) * (1.0 / OWN)
        column_sum = jnp.zeros((1, LANES), F32)
        cross = jnp.zeros((OBS, LANES), F32)
        for g in ARRIVAL:
            for n in range(g * SIDE, (g + 1) * SIDE):
                if n != SELF:
                    if f == 0:
                        wait_for(columns.at[:, 0 : EARLY * CHUNK, :], early_recv.at[n])
                    wait_for(columns.at[f, EARLY * CHUNK : OWN, :], col_recv.at[f, n])
            group = columns[f, g * GROUP : (g + 1) * GROUP, :]
            column_sum = column_sum + jnp.sum(group, axis=0, keepdims=True)
            cross = cross + dot_split(uth[g], utl[g], *split(group - near))
            if f == 0 and g == ARRIVAL[0]:
                h = jnp.broadcast_to(misfit * weight, (8, OBS))
                for _ in range(2):
                    h = p0 * h + dot_split(*split(dot_split(*split(h), *r_split)), *lifted_split)
                h_split = split(gain * h)
        centre = column_sum * (1.0 / MEMBERS)
        cross_split = split(cross)
        moved_split = split((root * scale * gain) * dot_split(*r_split, *cross_split))
        base = centre + dot_split(*h_split, *cross_split)[0:1, :]
        for g in range(SIDE):
            rows = slice(g * GROUP, (g + 1) * GROUP)
            shift = dot_split(uh[rows, :], ul[rows, :], *moved_split)
            result[f, rows, :] = base + (keep * (columns[f, rows, :] - centre) + shift)
            for n in range(g * SIDE, (g + 1) * SIDE):
                if n != SELF:
                    back_copy(n, f).start()
        returned[f, me] = result[f, block(SELF), :]

    finals = []
    for f in range(3):
        for half in range(2):
            for i in range(ROWS):
                src = 2 * i + half

                @pl.when(src != me)
                def _():
                    wait_for(returned.at[f, src], back_recv.at[f, src])

                for m in range(0, OWN, 8):
                    ready[half, pl.ds(m * LINES + f * ROWS + i, 8, stride=LINES), :] = returned[
                        f, src, m : m + 8, :
                    ]
            if f == 2:
                finals.append(
                    pltpu.make_async_copy(
                        ready.at[half], out.at[:, half * LANES : (half + 1) * LANES], out_sem.at[half]
                    )
                )
                finals[-1].start()
    for c in range(CHUNKS):
        halo_copy(c, 0).wait_send()
        halo_copy(c, 1).wait_send()
    for n in OTHERS:
        wait_for(seen, obs_send.at[n])
        wait_for(outgoing.at[:, 0, 0 : EARLY * CHUNK, :], early_send.at[n])
        for f in range(3):
            col_copy(n, f).wait_send()
            back_copy(n, f).wait_send()
    for k in range(1, N_TILE):
        sum_copy(k, lax.rem(tile + k, N_TILE)).wait_send()
    for copy in finals:
        copy.wait()


def on_device(ensemble, obs_cells, region_tile, obs_values, obs_error):
    state = ensemble.reshape(OWN * LINES, LONS)
    dma = pltpu.SemaphoreType.DMA
    updated = pl.pallas_call(
        kernel,
        name="analysis",
        out_shape=jax.ShapeDtypeStruct((OWN * LINES, LONS), F32),
        in_specs=[pl.BlockSpec(memory_space=pltpu.HBM)] * 5,
        out_specs=pl.BlockSpec(memory_space=pltpu.HBM),
        scratch_shapes=[
            pltpu.VMEM((N_TILE, OBS), jnp.int32),
            pltpu.SMEM((N_TILE,), jnp.int32),
            pltpu.VMEM((N_TILE, OBS), F32),
            pltpu.VMEM((N_TILE, OBS), F32),
            pltpu.VMEM((2, OWN * LINES, LANES), F32),
            pltpu.VMEM((3, ROWS + 2 * STEPS, OWN, LONS), F32),
            pltpu.VMEM((3, ROWS + 6, CHUNK, LONS), F32),
            pltpu.VMEM((3, ROWS + 4, CHUNK, LONS), F32),
            pltpu.VMEM((8, OBS), jnp.int32),
            pltpu.VMEM((8, OBS), jnp.int32),
            pltpu.VMEM((3, N_MEM, OWN, LANES), F32),
            pltpu.VMEM((OWN, OBS), F32),
            pltpu.VMEM((3, MEMBERS, LANES), F32),
            pltpu.VMEM((MEMBERS, OBS), F32),
            pltpu.VMEM((8, LANES), F32),
            pltpu.VMEM((N_TILE, 8, LANES), F32),
            pltpu.VMEM((SIDE, OBS, GROUP), BF16),
            pltpu.VMEM((SIDE, OBS, GROUP), BF16),
            pltpu.VMEM((MEMBERS, OBS), BF16),
            pltpu.VMEM((MEMBERS, OBS), BF16),
            pltpu.VMEM((3, MEMBERS, LANES), F32),
            pltpu.VMEM((3, N_MEM, OWN, LANES), F32),
            pltpu.VMEM((2, OWN * LINES, LANES), F32),
            dma((4,)),
            dma((CHUNKS, 2)),
            dma((2, CHUNKS)),
            dma((2, CHUNKS)),
            dma((N_MEM,)),
            dma((N_MEM,)),
            dma((N_MEM,)),
            dma((N_MEM,)),
            dma((3, N_MEM)),
            dma((3, N_MEM)),
            dma((N_TILE,)),
            dma((N_TILE,)),
            dma((3, N_MEM)),
            dma((3, N_MEM)),
            dma((2,)),
        ],
        compiler_params=pltpu.CompilerParams(
            collective_id=0, has_side_effects=True, vmem_limit_bytes=60_000_000
        ),
    )(state, obs_cells, region_tile, obs_values, obs_error)
    return updated.reshape(ensemble.shape)


def solution(mesh):
    in_specs = (P("mem", None, "tile", None), P(), P(), P(), P())
    out_specs = P("mem", None, "tile", None)
    return jax.shard_map(
        on_device, mesh=mesh, in_specs=in_specs, out_specs=out_specs, check_vma=False
    )
```

```python
import functools
import math

import jax
import jax.numpy as jnp
from jax import lax
from jax.experimental import pallas as pl
from jax.experimental.pallas import tpu as pltpu
from jax.sharding import PartitionSpec as P

MEMBERS = 1024
STEPS = 4
DEGREE = 4
SIDE = 4
N_MEM = 16
N_TILE = 16
ROWS = 8
LONS = 256
LANES = 128
OBS = 256
OWN = MEMBERS // N_MEM
LINES = 3 * ROWS
CHUNK = 8
CHUNKS = OWN // CHUNK
GROUP = SIDE * OWN

MESH = pl.DeviceIdType.MESH
F32, BF16 = jnp.float32, jnp.bfloat16

PARTNERS = [(dy, (dy + k) % SIDE) for k in (2, 1, 3, 0) for dy in (2, 1, 3, 0)]
BACK = [PARTNERS.index((-dy % SIDE, -dx % SIDE)) for dy, dx in PARTNERS]
OTHERS = range(N_MEM - 1)
SELF = N_MEM - 1
ARRIVAL = (0, 2, 1, 3)
EARLY = 2


def dot(a, b):
    return jnp.dot(a, b, preferred_element_type=F32)


def split(a):
    high = a.astype(BF16)
    return high, (a - high.astype(F32)).astype(BF16)


def dot_split(ah, al, bh, bl):
    return dot(ah, bh) + (dot(ah, bl) + dot(al, bh))


def matmul(a, b):
    return dot_split(*split(a), *split(b))


def total(a):
    return jnp.sum(jnp.sum(a, axis=0, keepdims=True), axis=1, keepdims=True)


def advanced(load):
    h, u, v = load(0, 1), load(1, 1), load(2, 1)
    hs, us, vs = load(0, 0), load(1, 0), load(2, 0)
    hn, un, vn = load(0, 2), load(1, 2), load(2, 2)
    he, hw = pltpu.roll(h, LONS - 1, 1), pltpu.roll(h, 1, 1)
    ue, uw = pltpu.roll(u, LONS - 1, 1), pltpu.roll(u, 1, 1)
    ve, vw = pltpu.roll(v, LONS - 1, 1), pltpu.roll(v, 1, 1)
    flux = ((1.0 + he) * ue - (1.0 + hw) * uw) + ((1.0 + hn) * vn - (1.0 + hs) * vs)
    push_u = u * (ue - uw) + v * (un - us) + (he - hw) - v
    push_v = u * (ve - vw) + v * (vn - vs) + (hn - hs) + u
    return (
        0.6 * h + 0.1 * ((he + hw) + (hn + hs)) - 0.15 * flux,
        0.6 * u + 0.1 * ((ue + uw) + (un + us)) - 0.15 * push_u,
        0.6 * v + 0.1 * ((ve + vw) + (vn + vs)) - 0.15 * push_v,
    )


def spectral_map(norm):
    bound = 2.0 + norm
    values = []
    for j in range(DEGREE + 1):
        angle = (j + 0.5) * (math.pi / (DEGREE + 1))
        values.append(lax.rsqrt(0.5 * (bound + 1.0) + (0.5 * math.cos(angle)) * (bound - 1.0)))
    coeffs = []
    for k in range(DEGREE + 1):
        factor = 2.0 / (DEGREE + 1) * (0.5 if k == 0 else 1.0)
        terms = [
            (factor * math.cos(k * (j + 0.5) * (math.pi / (DEGREE + 1)))) * values[j]
            for j in range(DEGREE + 1)
        ]
        coeffs.append(sum(terms[1:], terms[0]))
    return 2.0 / (bound - 1.0), coeffs


def kernel(
    state, cells_in, region_in, goals_in, errors_in, out,
    cells_ref, region_ref, goals_ref, errors_ref, raw, wide, ping, pong, slab_ref, lane_ref, outgoing, seen, columns, observed, sums_out, sums_in,
    uth, utl, uh, ul, result, returned, ready,
    small_sem, load_sem, halo_send, halo_recv, obs_send, obs_recv, early_send, early_recv, col_send, col_recv,
    sum_send, sum_recv, back_send, back_recv, out_sem,
):
    me = lax.axis_index("mem")
    tile = lax.axis_index("tile")
    mine_y, mine_x = me // SIDE, lax.rem(me, SIDE)
    above, below = lax.rem(tile + 1, N_TILE), lax.rem(tile + N_TILE - 1, N_TILE)

    def peer(n):
        dy, dx = PARTNERS[n]
        return lax.rem(mine_y + dy, SIDE) * SIDE + lax.rem(mine_x + dx, SIDE)

    def members(c):
        return pl.ds(pl.multiple_of(c * CHUNK, CHUNK), CHUNK)

    def block(n):
        return slice(n * OWN, (n + 1) * OWN)

    def load_copy(c):
        part = pl.ds(c * CHUNK * LINES, CHUNK * LINES)
        return [
            pltpu.make_async_copy(
                state.at[part, half * LANES : (half + 1) * LANES],
                raw.at[half, part, :],
                load_sem.at[c, half],
            )
            for half in range(2)
        ]

    def halo_copy(c, side):
        part = members(c)
        first, into, to = ((ROWS, 0, above), (STEPS, STEPS + ROWS, below))[side]
        return pltpu.make_async_remote_copy(
            src_ref=wide.at[:, first : first + STEPS, part, :],
            dst_ref=wide.at[:, into : into + STEPS, part, :],
            send_sem=halo_send.at[side, c],
            recv_sem=halo_recv.at[side, c],
            device_id={"tile": to},
            device_id_type=MESH,
        )

    def obs_copy(n, c, chunks):
        count = chunks * CHUNK
        first = pl.multiple_of(c * CHUNK, CHUNK)
        return pltpu.make_async_remote_copy(
            src_ref=seen.at[pl.ds(first, count), :],
            dst_ref=observed.at[pl.ds(BACK[n] * OWN + first, count), :],
            send_sem=obs_send.at[n],
            recv_sem=obs_recv.at[BACK[n]],
            device_id={"mem": peer(n)},
            device_id_type=MESH,
        )

    def early_copy(n, c):
        first = pl.multiple_of(c * CHUNK, CHUNK)
        return pltpu.make_async_remote_copy(
            src_ref=outgoing.at[:, peer(n), pl.ds(first, CHUNK), :],
            dst_ref=columns.at[:, pl.ds(BACK[n] * OWN + first, CHUNK), :],
            send_sem=early_send.at[n],
            recv_sem=early_recv.at[BACK[n]],
            device_id={"mem": peer(n)},
            device_id_type=MESH,
        )

    def col_copy(n, f):
        count = OWN - EARLY * CHUNK
        return pltpu.make_async_remote_copy(
            src_ref=outgoing.at[f, peer(n), pl.ds(EARLY * CHUNK, count), :],
            dst_ref=columns.at[f, pl.ds(BACK[n] * OWN + EARLY * CHUNK, count), :],
            send_sem=col_send.at[f, n],
            recv_sem=col_recv.at[f, BACK[n]],
            device_id={"mem": peer(n)},
            device_id_type=MESH,
        )

    def sum_copy(n, to):
        return pltpu.make_async_remote_copy(
            src_ref=sums_out,
            dst_ref=sums_in.at[tile],
            send_sem=sum_send.at[n],
            recv_sem=sum_recv.at[tile],
            device_id={"tile": to},
            device_id_type=MESH,
        )

    def back_copy(n, f):
        return pltpu.make_async_remote_copy(
            src_ref=result.at[f, block(n), :],
            dst_ref=returned.at[f, me],
            send_sem=back_send.at[f, n],
            recv_sem=back_recv.at[f, me],
            device_id={"mem": peer(n)},
            device_id_type=MESH,
        )

    def wait_for(ref, sem):
        pltpu.make_async_copy(ref, ref, sem).wait()

    small = [
        pltpu.make_async_copy(src, dst, small_sem.at[n])
        for n, (src, dst) in enumerate(
            [
                (region_in, region_ref),
                (cells_in, cells_ref),
                (goals_in, goals_ref),
                (errors_in, errors_ref),
            ]
        )
    ]
    for c in range(CHUNKS):
        for copy in load_copy(c):
            copy.start()
    for copy in small:
        copy.start()
    barrier = pltpu.get_barrier_semaphore()
    for n in OTHERS:
        pl.semaphore_signal(barrier, inc=1, device_id={"mem": peer(n)}, device_id_type=MESH)
    for k in range(1, N_TILE):
        to = lax.rem(tile + k, N_TILE)
        pl.semaphore_signal(barrier, inc=1, device_id={"tile": to}, device_id_type=MESH)

    for c in range(CHUNKS):
        for copy in load_copy(c):
            copy.wait()
        for m in range(c * CHUNK, (c + 1) * CHUNK, 8):
            for f in range(3):
                for i in range(ROWS):
                    first = m * LINES + f * ROWS + i
                    for half in range(2):
                        lanes = slice(half * LANES, (half + 1) * LANES)
                        wide[f, STEPS + i, m : m + 8, lanes] = raw[
                            half, pl.ds(first, 8, stride=LINES), :
                        ]
        if c == 0:
            pl.semaphore_wait(barrier, N_MEM + N_TILE - 2)
        halo_copy(c, 0).start()
        halo_copy(c, 1).start()

    for copy in small:
        copy.wait()
    cells = jnp.zeros((1, OBS), jnp.int32)
    goal = jnp.zeros((1, OBS), F32)
    error = jnp.zeros((1, OBS), F32)
    for region in range(N_TILE):
        chosen = region_ref[region] == tile
        cells = jnp.where(chosen, cells_ref[region : region + 1, :], cells)
        goal = jnp.where(chosen, goals_ref[region : region + 1, :], goal)
        error = jnp.where(chosen, errors_ref[region : region + 1, :], error)
    cells = jnp.broadcast_to(cells, (8, OBS))
    slab_ref[...] = lax.shift_right_logical(cells, 7)
    lane_ref[...] = lax.bitwise_and(cells, LANES - 1)

    def forecast(c, carry):
        part = members(c)
        wait_for(wide.at[:, 0:STEPS, part, :], halo_recv.at[0, c])
        wait_for(wide.at[:, 0:STEPS, part, :], halo_recv.at[1, c])

        def step(count, read, write):
            for i in range(count):
                new = advanced(lambda f, k: read(f, i + k))
                for f in range(3):
                    write[f, i] = new[f]

        step(ROWS + 6, lambda f, i: wide[f, i, part, :], ping)
        step(ROWS + 4, lambda f, i: ping[f, i], pong)
        step(ROWS + 2, lambda f, i: pong[f, i], ping)

        for i in range(ROWS):
            new = advanced(lambda f, k: ping[f, i + k])
            for f in range(3):
                for half in range(2):
                    lanes = slice(half * LANES, (half + 1) * LANES)
                    outgoing[f, 2 * i + half, part, :] = new[f][:, lanes]

        @pl.when(lax.rem(c, 2) == 1)
        def _():
            pair = pl.ds(pl.multiple_of((c - 1) * CHUNK, 2 * CHUNK), 2 * CHUNK)
            found = [[jnp.zeros((8, LANES), F32)] * 2 for _ in range(2)]
            for f in range(3):
                for j in range(2 * ROWS):
                    values = outgoing[f, j, pair, :]
                    for g in range(2):
                        lanes = slice(g * LANES, (g + 1) * LANES)
                        here = slab_ref[:, lanes] == f * (2 * ROWS) + j
                        for s in range(2):
                            taken = jnp.take_along_axis(
                                values[s * 8 : s * 8 + 8],
                                lane_ref[:, lanes],
                                axis=1,
                                mode="promise_in_bounds",
                            )
                            found[g][s] = jnp.where(here, taken, found[g][s])
            for g in range(2):
                lanes = slice(g * LANES, (g + 1) * LANES)
                seen[pair, lanes] = jnp.concatenate(found[g], axis=0)
            for n in OTHERS:
                obs_copy(n, c - 1, 2).start()

        @pl.when(c < EARLY)
        def _():
            for n in OTHERS:
                early_copy(n, c).start()

        return carry

    lax.fori_loop(0, CHUNKS, forecast, 0)
    for f in range(3):
        for n in OTHERS:
            col_copy(n, f).start()
    observed[block(SELF), :] = seen[...]
    columns[:, block(SELF), :] = outgoing[:, me]

    for n in OTHERS:
        wait_for(observed.at[block(n), :], obs_recv.at[n])
    obs_mean = jnp.sum(observed[...], axis=0, keepdims=True) * (1.0 / MEMBERS)
    weight = lax.rsqrt(error)
    misfit = goal - obs_mean
    square = jnp.zeros((1, OBS), F32)
    for b in range(SIDE):
        centred = observed[b * GROUP : (b + 1) * GROUP, :] - obs_mean
        square = square + jnp.sum(centred * centred, axis=0, keepdims=True)
    misfit_sum = total(misfit * misfit)
    spread_sum = total(square * (1.0 / (MEMBERS - 1)) + error)
    upper = lax.broadcasted_iota(jnp.int32, (8, LANES), 0) < 4
    sums_out[...] = jnp.where(upper, misfit_sum, spread_sum)
    for k in range(1, N_TILE):
        sum_copy(k, lax.rem(tile + k, N_TILE)).start()
    sums_in[tile] = sums_out[...]
    inner = jnp.zeros((OBS, OBS), F32)
    for b in range(SIDE):
        rows = slice(b * GROUP, (b + 1) * GROUP)
        scaled = (observed[rows, :] - obs_mean) * weight
        u_split = split(scaled)
        uh[rows, :], ul[rows, :] = u_split
        ut_split = split(scaled.T)
        uth[b], utl[b] = ut_split
        inner = inner + dot_split(*ut_split, *u_split)
    norm = jnp.sqrt(total(inner * inner))
    for k in range(1, N_TILE):
        src = lax.rem(tile + k, N_TILE)
        wait_for(sums_in.at[src], sum_recv.at[src])
    sums = jnp.sum(sums_in[...], axis=0)
    inflation = sums[0:1, 0:1] / sums[4:5, 0:1]

    gain = inflation * (1.0 / (MEMBERS - 1))
    root = jnp.sqrt(inflation)
    scale, c = spectral_map(gain * norm)
    p0 = c[0] - c[1] + c[2] - c[3] + c[4]
    eye = (
        lax.broadcasted_iota(jnp.int32, (OBS, OBS), 0)
        == lax.broadcasted_iota(jnp.int32, (OBS, OBS), 1)
    ).astype(F32)
    lifted = (scale * gain) * inner
    a = lifted - eye
    a_split = split(a)
    a2 = dot_split(*a_split, *a_split)
    a3 = dot_split(*split(a2), *a_split)
    r_split = split(
        c[1] * eye
        + (2.0 * c[2]) * (a - eye)
        + c[3] * (4.0 * (a2 - a) + eye)
        + (8.0 * c[4]) * (a3 - a2)
    )
    lifted_split = split(lifted)

    keep = root * p0
    for f in range(3):
        near = jnp.sum(outgoing[f, me], axis=0, keepdims=True) * (1.0 / OWN)
        column_sum = jnp.zeros((1, LANES), F32)
        cross = jnp.zeros((OBS, LANES), F32)
        for g in ARRIVAL:
            for n in range(g * SIDE, (g + 1) * SIDE):
                if n != SELF:
                    if f == 0:
                        wait_for(columns.at[:, 0 : EARLY * CHUNK, :], early_recv.at[n])
                    wait_for(columns.at[f, EARLY * CHUNK : OWN, :], col_recv.at[f, n])
            group = columns[f, g * GROUP : (g + 1) * GROUP, :]
            column_sum = column_sum + jnp.sum(group, axis=0, keepdims=True)
            cross = cross + dot_split(uth[g], utl[g], *split(group - near))
            if f == 0 and g == ARRIVAL[0]:
                h = jnp.broadcast_to(misfit * weight, (8, OBS))
                for _ in range(2):
                    h = p0 * h + dot_split(*split(dot_split(*split(h), *r_split)), *lifted_split)
                h_split = split(gain * h)
        centre = column_sum * (1.0 / MEMBERS)
        cross_split = split(cross)
        moved_split = split((root * scale * gain) * dot_split(*r_split, *cross_split))
        base = centre + dot_split(*h_split, *cross_split)[0:1, :]
        for g in range(SIDE):
            rows = slice(g * GROUP, (g + 1) * GROUP)
            shift = dot_split(uh[rows, :], ul[rows, :], *moved_split)
            result[f, rows, :] = base + (keep * (columns[f, rows, :] - centre) + shift)
            for n in range(g * SIDE, (g + 1) * SIDE):
                if n != SELF:
                    back_copy(n, f).start()
        returned[f, me] = result[f, block(SELF), :]

    finals = []
    for f in range(3):
        for half in range(2):
            for i in range(ROWS):
                src = 2 * i + half

                @pl.when(src != me)
                def _():
                    wait_for(returned.at[f, src], back_recv.at[f, src])

                for m in range(0, OWN, 8):
                    ready[half, pl.ds(m * LINES + f * ROWS + i, 8, stride=LINES), :] = returned[
                        f, src, m : m + 8, :
                    ]
            if f == 2:
                finals.append(
                    pltpu.make_async_copy(
                        ready.at[half], out.at[:, half * LANES : (half + 1) * LANES], out_sem.at[half]
                    )
                )
                finals[-1].start()
    for c in range(CHUNKS):
        halo_copy(c, 0).wait_send()
        halo_copy(c, 1).wait_send()
    for n in OTHERS:
        wait_for(seen, obs_send.at[n])
        wait_for(outgoing.at[:, 0, 0 : EARLY * CHUNK, :], early_send.at[n])
        for f in range(3):
            col_copy(n, f).wait_send()
            back_copy(n, f).wait_send()
    for k in range(1, N_TILE):
        sum_copy(k, lax.rem(tile + k, N_TILE)).wait_send()
    for copy in finals:
        copy.wait()


def on_device(ensemble, obs_cells, region_tile, obs_values, obs_error):
    state = ensemble.reshape(OWN * LINES, LONS)
    dma = pltpu.SemaphoreType.DMA
    updated = pl.pallas_call(
        kernel,
        name="analysis",
        out_shape=jax.ShapeDtypeStruct((OWN * LINES, LONS), F32),
        in_specs=[pl.BlockSpec(memory_space=pltpu.HBM)] * 5,
        out_specs=pl.BlockSpec(memory_space=pltpu.HBM),
        scratch_shapes=[
            pltpu.VMEM((N_TILE, OBS), jnp.int32),
            pltpu.SMEM((N_TILE,), jnp.int32),
            pltpu.VMEM((N_TILE, OBS), F32),
            pltpu.VMEM((N_TILE, OBS), F32),
            pltpu.VMEM((2, OWN * LINES, LANES), F32),
            pltpu.VMEM((3, ROWS + 2 * STEPS, OWN, LONS), F32),
            pltpu.VMEM((3, ROWS + 6, CHUNK, LONS), F32),
            pltpu.VMEM((3, ROWS + 4, CHUNK, LONS), F32),
            pltpu.VMEM((8, OBS), jnp.int32),
            pltpu.VMEM((8, OBS), jnp.int32),
            pltpu.VMEM((3, N_MEM, OWN, LANES), F32),
            pltpu.VMEM((OWN, OBS), F32),
            pltpu.VMEM((3, MEMBERS, LANES), F32),
            pltpu.VMEM((MEMBERS, OBS), F32),
            pltpu.VMEM((8, LANES), F32),
            pltpu.VMEM((N_TILE, 8, LANES), F32),
            pltpu.VMEM((SIDE, OBS, GROUP), BF16),
            pltpu.VMEM((SIDE, OBS, GROUP), BF16),
            pltpu.VMEM((MEMBERS, OBS), BF16),
            pltpu.VMEM((MEMBERS, OBS), BF16),
            pltpu.VMEM((3, MEMBERS, LANES), F32),
            pltpu.VMEM((3, N_MEM, OWN, LANES), F32),
            pltpu.VMEM((2, OWN * LINES, LANES), F32),
            dma((4,)),
            dma((CHUNKS, 2)),
            dma((2, CHUNKS)),
            dma((2, CHUNKS)),
            dma((N_MEM,)),
            dma((N_MEM,)),
            dma((N_MEM,)),
            dma((N_MEM,)),
            dma((3, N_MEM)),
            dma((3, N_MEM)),
            dma((N_TILE,)),
            dma((N_TILE,)),
            dma((3, N_MEM)),
            dma((3, N_MEM)),
            dma((2,)),
        ],
        compiler_params=pltpu.CompilerParams(
            collective_id=0, has_side_effects=True, vmem_limit_bytes=60_000_000
        ),
    )(state, obs_cells, region_tile, obs_values, obs_error)
    return updated.reshape(ensemble.shape)


def solution(mesh):
    in_specs = (P("mem", None, "tile", None), P(), P(), P(), P())
    out_specs = P("mem", None, "tile", None)
    return jax.shard_map(
        on_device, mesh=mesh, in_specs=in_specs, out_specs=out_specs, check_vma=False
    )
```

```python
import functools
import math

import jax
import jax.numpy as jnp
from jax import lax
from jax.experimental import pallas as pl
from jax.experimental.pallas import tpu as pltpu
from jax.sharding import PartitionSpec as P

MEMBERS = 1024
STEPS = 4
DEGREE = 4
SIDE = 4
N_MEM = 16
N_TILE = 16
ROWS = 8
LONS = 256
LANES = 128
OBS = 256
OWN = MEMBERS // N_MEM
LINES = 3 * ROWS
CHUNK = 8
CHUNKS = OWN // CHUNK
GROUP = SIDE * OWN

MESH = pl.DeviceIdType.MESH
F32, BF16 = jnp.float32, jnp.bfloat16

PARTNERS = [(dy, (dy + k) % SIDE) for k in (2, 1, 3, 0) for dy in (2, 1, 3, 0)]
BACK = [PARTNERS.index((-dy % SIDE, -dx % SIDE)) for dy, dx in PARTNERS]
OTHERS = range(N_MEM - 1)
ALTERNATING = [(0, 1), (1, 0), (0, 3), (3, 0), (0, 2), (2, 0), (1, 1), (3, 3)]
ALTERNATING += [(3, 1), (1, 3), (1, 2), (2, 1), (3, 2), (2, 3), (2, 2)]
SENDS = [PARTNERS.index(offset) for offset in ALTERNATING]
SELF = N_MEM - 1
ARRIVAL = (0, 2, 1, 3)
EARLY = 2


def dot(a, b):
    return jnp.dot(a, b, preferred_element_type=F32)


def split(a):
    high = a.astype(BF16)
    return high, (a - high.astype(F32)).astype(BF16)


def dot_split(ah, al, bh, bl):
    return dot(ah, bh) + (dot(ah, bl) + dot(al, bh))


def matmul(a, b):
    return dot_split(*split(a), *split(b))


def total(a):
    return jnp.sum(jnp.sum(a, axis=0, keepdims=True), axis=1, keepdims=True)


def advanced(load):
    h, u, v = load(0, 1), load(1, 1), load(2, 1)
    hs, us, vs = load(0, 0), load(1, 0), load(2, 0)
    hn, un, vn = load(0, 2), load(1, 2), load(2, 2)
    he, hw = pltpu.roll(h, LONS - 1, 1), pltpu.roll(h, 1, 1)
    ue, uw = pltpu.roll(u, LONS - 1, 1), pltpu.roll(u, 1, 1)
    ve, vw = pltpu.roll(v, LONS - 1, 1), pltpu.roll(v, 1, 1)
    flux = ((1.0 + he) * ue - (1.0 + hw) * uw) + ((1.0 + hn) * vn - (1.0 + hs) * vs)
    push_u = u * (ue - uw) + v * (un - us) + (he - hw) - v
    push_v = u * (ve - vw) + v * (vn - vs) + (hn - hs) + u
    return (
        0.6 * h + 0.1 * ((he + hw) + (hn + hs)) - 0.15 * flux,
        0.6 * u + 0.1 * ((ue + uw) + (un + us)) - 0.15 * push_u,
        0.6 * v + 0.1 * ((ve + vw) + (vn + vs)) - 0.15 * push_v,
    )


def spectral_map(norm):
    bound = 2.0 + norm
    values = []
    for j in range(DEGREE + 1):
        angle = (j + 0.5) * (math.pi / (DEGREE + 1))
        values.append(lax.rsqrt(0.5 * (bound + 1.0) + (0.5 * math.cos(angle)) * (bound - 1.0)))
    coeffs = []
    for k in range(DEGREE + 1):
        factor = 2.0 / (DEGREE + 1) * (0.5 if k == 0 else 1.0)
        terms = [
            (factor * math.cos(k * (j + 0.5) * (math.pi / (DEGREE + 1)))) * values[j]
            for j in range(DEGREE + 1)
        ]
        coeffs.append(sum(terms[1:], terms[0]))
    return 2.0 / (bound - 1.0), coeffs


def kernel(
    state, cells_in, region_in, goals_in, errors_in, out,
    cells_ref, region_ref, goals_ref, errors_ref, raw, wide, ping, pong, slab_ref, lane_ref, outgoing, seen, columns, observed, sums_out, sums_in,
    uth, utl, uh, ul, result, returned, ready,
    small_sem, load_sem, halo_send, halo_recv, obs_send, obs_recv, early_send, early_recv, col_send, col_recv,
    sum_send, sum_recv, back_send, back_recv, out_sem,
):
    me = lax.axis_index("mem")
    tile = lax.axis_index("tile")
    mine_y, mine_x = me // SIDE, lax.rem(me, SIDE)
    above, below = lax.rem(tile + 1, N_TILE), lax.rem(tile + N_TILE - 1, N_TILE)

    def peer(n):
        dy, dx = PARTNERS[n]
        return lax.rem(mine_y + dy, SIDE) * SIDE + lax.rem(mine_x + dx, SIDE)

    def members(c):
        return pl.ds(pl.multiple_of(c * CHUNK, CHUNK), CHUNK)

    def block(n):
        return slice(n * OWN, (n + 1) * OWN)

    def load_copy(c):
        part = pl.ds(c * CHUNK * LINES, CHUNK * LINES)
        return [
            pltpu.make_async_copy(
                state.at[part, half * LANES : (half + 1) * LANES],
                raw.at[half, part, :],
                load_sem.at[c, half],
            )
            for half in range(2)
        ]

    def halo_copy(c, side):
        part = members(c)
        first, into, to = ((ROWS, 0, above), (STEPS, STEPS + ROWS, below))[side]
        return pltpu.make_async_remote_copy(
            src_ref=wide.at[:, first : first + STEPS, part, :],
            dst_ref=wide.at[:, into : into + STEPS, part, :],
            send_sem=halo_send.at[side, c],
            recv_sem=halo_recv.at[side, c],
            device_id={"tile": to},
            device_id_type=MESH,
        )

    def obs_copy(n, c, chunks):
        count = chunks * CHUNK
        first = pl.multiple_of(c * CHUNK, CHUNK)
        return pltpu.make_async_remote_copy(
            src_ref=seen.at[pl.ds(first, count), :],
            dst_ref=observed.at[pl.ds(BACK[n] * OWN + first, count), :],
            send_sem=obs_send.at[n],
            recv_sem=obs_recv.at[BACK[n]],
            device_id={"mem": peer(n)},
            device_id_type=MESH,
        )

    def early_copy(n, c):
        first = pl.multiple_of(c * CHUNK, CHUNK)
        return pltpu.make_async_remote_copy(
            src_ref=outgoing.at[:, peer(n), pl.ds(first, CHUNK), :],
            dst_ref=columns.at[:, pl.ds(BACK[n] * OWN + first, CHUNK), :],
            send_sem=early_send.at[n],
            recv_sem=early_recv.at[BACK[n]],
            device_id={"mem": peer(n)},
            device_id_type=MESH,
        )

    def col_copy(n, f):
        count = OWN - EARLY * CHUNK
        return pltpu.make_async_remote_copy(
            src_ref=outgoing.at[f, peer(n), pl.ds(EARLY * CHUNK, count), :],
            dst_ref=columns.at[f, pl.ds(BACK[n] * OWN + EARLY * CHUNK, count), :],
            send_sem=col_send.at[f, n],
            recv_sem=col_recv.at[f, BACK[n]],
            device_id={"mem": peer(n)},
            device_id_type=MESH,
        )

    def sum_copy(n, to):
        return pltpu.make_async_remote_copy(
            src_ref=sums_out,
            dst_ref=sums_in.at[tile],
            send_sem=sum_send.at[n],
            recv_sem=sum_recv.at[tile],
            device_id={"tile": to},
            device_id_type=MESH,
        )

    def back_copy(n, f):
        return pltpu.make_async_remote_copy(
            src_ref=result.at[f, block(n), :],
            dst_ref=returned.at[f, me],
            send_sem=back_send.at[f, n],
            recv_sem=back_recv.at[f, me],
            device_id={"mem": peer(n)},
            device_id_type=MESH,
        )

    def wait_for(ref, sem):
        pltpu.make_async_copy(ref, ref, sem).wait()

    small = [
        pltpu.make_async_copy(src, dst, small_sem.at[n])
        for n, (src, dst) in enumerate(
            [
                (region_in, region_ref),
                (cells_in, cells_ref),
                (goals_in, goals_ref),
                (errors_in, errors_ref),
            ]
        )
    ]
    for c in range(CHUNKS):
        for copy in load_copy(c):
            copy.start()
    for copy in small:
        copy.start()
    barrier = pltpu.get_barrier_semaphore()
    for n in OTHERS:
        pl.semaphore_signal(barrier, inc=1, device_id={"mem": peer(n)}, device_id_type=MESH)
    for k in range(1, N_TILE):
        to = lax.rem(tile + k, N_TILE)
        pl.semaphore_signal(barrier, inc=1, device_id={"tile": to}, device_id_type=MESH)

    for c in range(CHUNKS):
        for copy in load_copy(c):
            copy.wait()
        for m in range(c * CHUNK, (c + 1) * CHUNK, 8):
            for f in range(3):
                for i in range(ROWS):
                    first = m * LINES + f * ROWS + i
                    for half in range(2):
                        lanes = slice(half * LANES, (half + 1) * LANES)
                        wide[f, STEPS + i, m : m + 8, lanes] = raw[
                            half, pl.ds(first, 8, stride=LINES), :
                        ]
        if c == 0:
            pl.semaphore_wait(barrier, N_MEM + N_TILE - 2)
        halo_copy(c, 0).start()
        halo_copy(c, 1).start()

    for copy in small:
        copy.wait()
    cells = jnp.zeros((1, OBS), jnp.int32)
    goal = jnp.zeros((1, OBS), F32)
    error = jnp.zeros((1, OBS), F32)
    for region in range(N_TILE):
        chosen = region_ref[region] == tile
        cells = jnp.where(chosen, cells_ref[region : region + 1, :], cells)
        goal = jnp.where(chosen, goals_ref[region : region + 1, :], goal)
        error = jnp.where(chosen, errors_ref[region : region + 1, :], error)
    cells = jnp.broadcast_to(cells, (8, OBS))
    slab_ref[...] = lax.shift_right_logical(cells, 7)
    lane_ref[...] = lax.bitwise_and(cells, LANES - 1)

    def forecast(c, carry):
        part = members(c)
        wait_for(wide.at[:, 0:STEPS, part, :], halo_recv.at[0, c])
        wait_for(wide.at[:, 0:STEPS, part, :], halo_recv.at[1, c])

        def step(count, read, write):
            for i in range(count):
                new = advanced(lambda f, k: read(f, i + k))
                for f in range(3):
                    write[f, i] = new[f]

        step(ROWS + 6, lambda f, i: wide[f, i, part, :], ping)
        step(ROWS + 4, lambda f, i: ping[f, i], pong)
        step(ROWS + 2, lambda f, i: pong[f, i], ping)

        for i in range(ROWS):
            new = advanced(lambda f, k: ping[f, i + k])
            for f in range(3):
                for half in range(2):
                    lanes = slice(half * LANES, (half + 1) * LANES)
                    outgoing[f, 2 * i + half, part, :] = new[f][:, lanes]

        @pl.when(lax.rem(c, 2) == 1)
        def _():
            pair = pl.ds(pl.multiple_of((c - 1) * CHUNK, 2 * CHUNK), 2 * CHUNK)
            found = [[jnp.zeros((8, LANES), F32)] * 2 for _ in range(2)]
            for f in range(3):
                for j in range(2 * ROWS):
                    values = outgoing[f, j, pair, :]
                    for g in range(2):
                        lanes = slice(g * LANES, (g + 1) * LANES)
                        here = slab_ref[:, lanes] == f * (2 * ROWS) + j
                        for s in range(2):
                            taken = jnp.take_along_axis(
                                values[s * 8 : s * 8 + 8],
                                lane_ref[:, lanes],
                                axis=1,
                                mode="promise_in_bounds",
                            )
                            found[g][s] = jnp.where(here, taken, found[g][s])
            for g in range(2):
                lanes = slice(g * LANES, (g + 1) * LANES)
                seen[pair, lanes] = jnp.concatenate(found[g], axis=0)
            for n in SENDS:
                obs_copy(n, c - 1, 2).start()

        @pl.when(c < EARLY)
        def _():
            for n in SENDS:
                early_copy(n, c).start()

        return carry

    lax.fori_loop(0, CHUNKS, forecast, 0)
    for f in range(3):
        for n in SENDS:
            col_copy(n, f).start()
    observed[block(SELF), :] = seen[...]
    columns[:, block(SELF), :] = outgoing[:, me]

    for n in OTHERS:
        wait_for(observed.at[block(n), :], obs_recv.at[n])
    obs_mean = jnp.sum(observed[...], axis=0, keepdims=True) * (1.0 / MEMBERS)
    weight = lax.rsqrt(error)
    misfit = goal - obs_mean
    square = jnp.zeros((1, OBS), F32)
    for b in range(SIDE):
        centred = observed[b * GROUP : (b + 1) * GROUP, :] - obs_mean
        square = square + jnp.sum(centred * centred, axis=0, keepdims=True)
    misfit_sum = total(misfit * misfit)
    spread_sum = total(square * (1.0 / (MEMBERS - 1)) + error)
    upper = lax.broadcasted_iota(jnp.int32, (8, LANES), 0) < 4
    sums_out[...] = jnp.where(upper, misfit_sum, spread_sum)
    for k in range(1, N_TILE):
        sum_copy(k, lax.rem(tile + k, N_TILE)).start()
    sums_in[tile] = sums_out[...]
    inner = jnp.zeros((OBS, OBS), F32)
    for b in range(SIDE):
        rows = slice(b * GROUP, (b + 1) * GROUP)
        scaled = (observed[rows, :] - obs_mean) * weight
        u_split = split(scaled)
        uh[rows, :], ul[rows, :] = u_split
        ut_split = split(scaled.T)
        uth[b], utl[b] = ut_split
        inner = inner + dot_split(*ut_split, *u_split)
    norm = jnp.sqrt(total(inner * inner))
    for k in range(1, N_TILE):
        src = lax.rem(tile + k, N_TILE)
        wait_for(sums_in.at[src], sum_recv.at[src])
    sums = jnp.sum(sums_in[...], axis=0)
    inflation = sums[0:1, 0:1] / sums[4:5, 0:1]

    gain = inflation * (1.0 / (MEMBERS - 1))
    root = jnp.sqrt(inflation)
    scale, c = spectral_map(gain * norm)
    p0 = c[0] - c[1] + c[2] - c[3] + c[4]
    eye = (
        lax.broadcasted_iota(jnp.int32, (OBS, OBS), 0)
        == lax.broadcasted_iota(jnp.int32, (OBS, OBS), 1)
    ).astype(F32)
    lifted = (scale * gain) * inner
    a = lifted - eye
    a_split = split(a)
    a2 = dot_split(*a_split, *a_split)
    a3 = dot_split(*split(a2), *a_split)
    r_split = split(
        c[1] * eye
        + (2.0 * c[2]) * (a - eye)
        + c[3] * (4.0 * (a2 - a) + eye)
        + (8.0 * c[4]) * (a3 - a2)
    )
    lifted_split = split(lifted)

    keep = root * p0
    for f in range(3):
        near = jnp.sum(outgoing[f, me], axis=0, keepdims=True) * (1.0 / OWN)
        column_sum = jnp.zeros((1, LANES), F32)
        cross = jnp.zeros((OBS, LANES), F32)
        for g in ARRIVAL:
            for n in range(g * SIDE, (g + 1) * SIDE):
                if n != SELF:
                    if f == 0:
                        wait_for(columns.at[:, 0 : EARLY * CHUNK, :], early_recv.at[n])
                    wait_for(columns.at[f, EARLY * CHUNK : OWN, :], col_recv.at[f, n])
            group = columns[f, g * GROUP : (g + 1) * GROUP, :]
            column_sum = column_sum + jnp.sum(group, axis=0, keepdims=True)
            cross = cross + dot_split(uth[g], utl[g], *split(group - near))
            if f == 0 and g == ARRIVAL[0]:
                h = jnp.broadcast_to(misfit * weight, (8, OBS))
                for _ in range(2):
                    h = p0 * h + dot_split(*split(dot_split(*split(h), *r_split)), *lifted_split)
                h_split = split(gain * h)
        centre = column_sum * (1.0 / MEMBERS)
        cross_split = split(cross)
        moved_split = split((root * scale * gain) * dot_split(*r_split, *cross_split))
        base = centre + dot_split(*h_split, *cross_split)[0:1, :]
        for g in range(SIDE):
            rows = slice(g * GROUP, (g + 1) * GROUP)
            shift = dot_split(uh[rows, :], ul[rows, :], *moved_split)
            result[f, rows, :] = base + (keep * (columns[f, rows, :] - centre) + shift)
            for n in range(g * SIDE, (g + 1) * SIDE):
                if n != SELF:
                    back_copy(n, f).start()
        returned[f, me] = result[f, block(SELF), :]

    finals = []
    for f in range(3):
        for half in range(2):
            for i in range(ROWS):
                src = 2 * i + half

                @pl.when(src != me)
                def _():
                    wait_for(returned.at[f, src], back_recv.at[f, src])

                for m in range(0, OWN, 8):
                    ready[half, pl.ds(m * LINES + f * ROWS + i, 8, stride=LINES), :] = returned[
                        f, src, m : m + 8, :
                    ]
            if f == 2:
                finals.append(
                    pltpu.make_async_copy(
                        ready.at[half], out.at[:, half * LANES : (half + 1) * LANES], out_sem.at[half]
                    )
                )
                finals[-1].start()
    for c in range(CHUNKS):
        halo_copy(c, 0).wait_send()
        halo_copy(c, 1).wait_send()
    for n in OTHERS:
        wait_for(seen, obs_send.at[n])
        wait_for(outgoing.at[:, 0, 0 : EARLY * CHUNK, :], early_send.at[n])
        for f in range(3):
            col_copy(n, f).wait_send()
            back_copy(n, f).wait_send()
    for k in range(1, N_TILE):
        sum_copy(k, lax.rem(tile + k, N_TILE)).wait_send()
    for copy in finals:
        copy.wait()


def on_device(ensemble, obs_cells, region_tile, obs_values, obs_error):
    state = ensemble.reshape(OWN * LINES, LONS)
    dma = pltpu.SemaphoreType.DMA
    updated = pl.pallas_call(
        kernel,
        name="analysis",
        out_shape=jax.ShapeDtypeStruct((OWN * LINES, LONS), F32),
        in_specs=[pl.BlockSpec(memory_space=pltpu.HBM)] * 5,
        out_specs=pl.BlockSpec(memory_space=pltpu.HBM),
        scratch_shapes=[
            pltpu.VMEM((N_TILE, OBS), jnp.int32),
            pltpu.SMEM((N_TILE,), jnp.int32),
            pltpu.VMEM((N_TILE, OBS), F32),
            pltpu.VMEM((N_TILE, OBS), F32),
            pltpu.VMEM((2, OWN * LINES, LANES), F32),
            pltpu.VMEM((3, ROWS + 2 * STEPS, OWN, LONS), F32),
            pltpu.VMEM((3, ROWS + 6, CHUNK, LONS), F32),
            pltpu.VMEM((3, ROWS + 4, CHUNK, LONS), F32),
            pltpu.VMEM((8, OBS), jnp.int32),
            pltpu.VMEM((8, OBS), jnp.int32),
            pltpu.VMEM((3, N_MEM, OWN, LANES), F32),
            pltpu.VMEM((OWN, OBS), F32),
            pltpu.VMEM((3, MEMBERS, LANES), F32),
            pltpu.VMEM((MEMBERS, OBS), F32),
            pltpu.VMEM((8, LANES), F32),
            pltpu.VMEM((N_TILE, 8, LANES), F32),
            pltpu.VMEM((SIDE, OBS, GROUP), BF16),
            pltpu.VMEM((SIDE, OBS, GROUP), BF16),
            pltpu.VMEM((MEMBERS, OBS), BF16),
            pltpu.VMEM((MEMBERS, OBS), BF16),
            pltpu.VMEM((3, MEMBERS, LANES), F32),
            pltpu.VMEM((3, N_MEM, OWN, LANES), F32),
            pltpu.VMEM((2, OWN * LINES, LANES), F32),
            dma((4,)),
            dma((CHUNKS, 2)),
            dma((2, CHUNKS)),
            dma((2, CHUNKS)),
            dma((N_MEM,)),
            dma((N_MEM,)),
            dma((N_MEM,)),
            dma((N_MEM,)),
            dma((3, N_MEM)),
            dma((3, N_MEM)),
            dma((N_TILE,)),
            dma((N_TILE,)),
            dma((3, N_MEM)),
            dma((3, N_MEM)),
            dma((2,)),
        ],
        compiler_params=pltpu.CompilerParams(
            collective_id=0, has_side_effects=True, vmem_limit_bytes=60_000_000
        ),
    )(state, obs_cells, region_tile, obs_values, obs_error)
    return updated.reshape(ensemble.shape)


def solution(mesh):
    in_specs = (P("mem", None, "tile", None), P(), P(), P(), P())
    out_specs = P("mem", None, "tile", None)
    return jax.shard_map(
        on_device, mesh=mesh, in_specs=in_specs, out_specs=out_specs, check_vma=False
    )
```
